256 devices in a mesh: freq: 16 (over x_lo, y, core), gz: 16 (over x_hi, z).
Axes of the slice: x: 4 (x_hi: 2, x_lo: 2; x = x_hi * 2 + x_lo), y: 4, z: 8, core: 2. Of those that a mesh axis runs over, the one named last changes fastest.
Arguments:
- displacement: float32 [16, 2, 3, 64, 64, 128], P('freq', None, None, 'gz'), may hold values from -6 to 6
- freq_index: int32 [16], P('freq'), may hold values from 0 to 7
- tissue: int32 [64, 64, 128], P('gz'), may hold values from 0 to 1, as said below
Outputs:
- modulus: float32 [2, 64, 64, 128], P(None, 'gz')
- residual: float32 [2, 64, 64, 128], P(None, 'gz')
The draws below stay inside these ranges and needn't reach their ends.
Inputs may be any that keep to these rules, and one draw needn't show every extreme that they name: 0 outside tissue, 1 inside; the share of tissue rises along z from about 0.15 to about 0.95.
All inputs are finite; a program needn't handle non-finite values.
Results may differ from the reference program's by a relative error of at most 0.0003.
Values sent between devices are 32-bit elements; how exact they have to be, the bound alone decides.
No kernel may reach another device: no remote copies, remote signals or barrier semaphores. Data moves between devices by JAX's collectives and lax.ppermute only.
A program may use at most 64 MiB of HBM per device.

```python
import jax
import jax.numpy as jnp
from jax import lax

NY = 64
NX = 128
ITERS = 2
FREQ_COUNT = 8
GROUPS = 16
NZ = 64


def draw_tissue(key, part):
    depth = lax.broadcasted_iota(jnp.int32, (NZ, NY, NX), 0)
    level = 150 + 800 * depth // NZ
    rolled = jax.random.randint(key, (NZ, NY, NX), 0, 1000)
    return (rolled < level).astype(jnp.int32)


def place_ends(drawn, own_key, low, high):
    spot = [jax.random.randint(jax.random.fold_in(own_key, axis), (), 0, length) for axis, length in enumerate(drawn.shape)]
    main_axis = drawn.shape.index(max(drawn.shape))
    neighbour = spot[:main_axis] + [(spot[main_axis] + 1) % drawn.shape[main_axis]] + spot[main_axis + 1:]
    return drawn.at[tuple(spot)].set(low).at[tuple(neighbour)].set(high)


def block_levels(stream_key, dims, shards, least, largest):
    gain, own = 1.0, jax.random.fold_in(stream_key, 6)
    for position, blocks in shards:
        steps = jnp.exp(jax.random.uniform(jax.random.fold_in(own, position), (blocks,), jnp.float32, least / len(shards), largest / len(shards)))
        gain = gain * jnp.repeat(steps, dims[position] // blocks).reshape([-1 if axis == position else 1 for axis in range(len(dims))])
    return gain


def noise(rng, dims, deviation, bound, shards=(), kind=jnp.bfloat16):
    entries = deviation * jax.random.normal(rng, dims, jnp.float32)
    if shards:
        entries = entries * block_levels(rng, dims, shards, -0.22, 0.18)
    return jnp.clip(entries, -bound, bound).astype(kind)


def setup_inputs(seed: int = 0) -> dict:
    key_list = jax.random.split(jax.random.key(seed), 4)
    return {
        "displacement": noise(key_list[0], (GROUPS, 2, 3, NZ, NY, NX), 1.0, 6.0, ((0, 16), (3, 16)), jnp.float32),
        "freq_index": place_ends(jax.random.randint(key_list[1], (GROUPS,), 0, FREQ_COUNT), jax.random.fold_in(key_list[1], 1), 0, FREQ_COUNT - 1).astype(jnp.int32),
        "tissue": draw_tissue(jax.random.fold_in(key_list[3], 71), 0),
    }


DAMPING = 0.05


def zero_plane(field, spatial):
    return jnp.zeros_like(lax.slice_in_dim(field, 0, 1, axis=spatial))


def ahead(field, spatial, tail):
    moved = lax.slice_in_dim(field, 1, field.shape[spatial], axis=spatial)
    return jnp.concatenate([moved, tail], axis=spatial)


def behind(field, spatial, head):
    moved = lax.slice_in_dim(field, 0, field.shape[spatial] - 1, axis=spatial)
    return jnp.concatenate([head, moved], axis=spatial)


def gradients(field):
    return [ahead(field, spatial, zero_plane(field, spatial)) - field for spatial in (2, 3, 4)]


def forward(modulus, grads):
    total = None
    for spatial, grad in zip((2, 3, 4), grads):
        real = modulus[0] * grad[0] - modulus[1] * grad[1]
        imag = modulus[0] * grad[1] + modulus[1] * grad[0]
        flux = jnp.stack([real, imag])
        term = flux - behind(flux, spatial, zero_plane(flux, spatial))
        total = term if total is None else total + term
    return total


def adjoint(values, grads):
    real = None
    imag = None
    for spatial, grad in zip((2, 3, 4), grads):
        diff = values - ahead(values, spatial, zero_plane(values, spatial))
        part_real = jnp.sum(grad[0] * diff[0] + grad[1] * diff[1], axis=0)
        part_imag = jnp.sum(grad[0] * diff[1] - grad[1] * diff[0], axis=0)
        real = part_real if real is None else real + part_real
        imag = part_imag if imag is None else imag + part_imag
    return jnp.stack([real, imag])


def reference(displacement, freq_index, tissue):
    weight = tissue.astype(jnp.float32)
    empty = jnp.zeros((2, NZ, NY, NX), jnp.float32)

    def right_group(carry, item):
        field, index = item
        grads = gradients(field)
        kappa = 0.2 * (index + 1).astype(jnp.float32)
        return carry + adjoint(weight * (-kappa * field), grads), None

    def normal_apply(direction):
        def one_group(carry, item):
            field, index = item
            grads = gradients(field)
            return carry + adjoint(weight * forward(direction, grads), grads), None

        total, _ = lax.scan(one_group, empty, (displacement, freq_index))
        return total + DAMPING * direction

    right, _ = lax.scan(right_group, empty, (displacement, freq_index))
    modulus = empty
    residual = right
    direction = right
    norm_now = jnp.sum(residual * residual)
    for iteration in range(ITERS):
        image = normal_apply(direction)
        step_size = norm_now / jnp.sum(direction * image)
        modulus = modulus + step_size * direction
        residual = residual - step_size * image
        norm_next = jnp.sum(residual * residual)
        direction = residual + (norm_next / norm_now) * direction
        norm_now = norm_next
    return modulus, residual
```

```python
import jax
import jax.numpy as jnp
from jax import lax
from jax.sharding import PartitionSpec as P

DAMPING = 0.05
ROWS = 8


def swap_cores(array):
    pairs = [(i, i ^ 1) for i in range(lax.axis_size("freq"))]
    return lax.ppermute(array, "freq", pairs)


def to_slabs(array, first_up, cross):
    peers, slabs = lax.axis_size("freq"), lax.axis_size("gz")
    pairs = []
    for f in range(peers):
        for g in range(slabs):
            to = g + 1 if f % 2 == first_up else g - 1
            if 0 <= to < slabs:
                pairs.append((f * slabs + g, (f ^ cross) * slabs + to))
    return lax.ppermute(array, ("freq", "gz"), pairs)


def over_chips(parts):
    peers = lax.axis_size("freq")
    groups = [list(range(core, peers, 2)) for core in range(2)]
    return lax.all_to_all(parts, "freq", split_axis=0, concat_axis=0, tiled=True, axis_index_groups=groups)


def nxt(field, dim):
    dim = dim % field.ndim
    pad = [(0, 0)] * field.ndim
    pad[dim] = (0, 1)
    return lax.slice_in_dim(jnp.pad(field, pad), 1, field.shape[dim] + 1, axis=dim)


def prv(field, dim):
    dim = dim % field.ndim
    pad = [(0, 0)] * field.ndim
    pad[dim] = (1, 0)
    return lax.slice_in_dim(jnp.pad(field, pad), 0, field.shape[dim], axis=dim)


def herm(a, b):
    real = jnp.sum(a[:, 0] * b[:, 0] + a[:, 1] * b[:, 1], axis=(0, 1))
    imag = jnp.sum(a[:, 0] * b[:, 1] - a[:, 1] * b[:, 0], axis=(0, 1))
    return real, imag


def square(a):
    return jnp.sum(a * a, axis=(0, 1, 2))


def stencil(field, kappa, mask):
    own = field[:, :, :, 1:3]
    gz = field[:, :, :, 1:] - field[:, :, :, :-1]
    gy = nxt(own, -2) - own
    gx = nxt(own, -1) - own
    here = mask[:2]
    gz_own, gz_prv = gz[:, :, :, 1:], gz[:, :, :, :-1]
    total = gz_own + gy + gx
    gy_prv, gx_prv = prv(gy, -2), prv(gx, -1)
    my, mx = nxt(here, -2), nxt(here, -1)
    diag = here * square(total) + mask[1:] * square(gz_own) + my * square(gy) + mx * square(gx)
    rows = [diag]
    for other in (gz_prv, gy_prv, gx_prv):
        rows += [-here * part for part in herm(total, other)]
    for one, two in ((gz_prv, gy_prv), (gz_prv, gx_prv), (gy_prv, gx_prv)):
        rows += [here * part for part in herm(one, two)]
    scaled = -kappa[:, None, None, None, None, None] * field[:, :, :, 1:]
    target = scaled * mask
    mine = target[:, :, :, :2]
    right = [jnp.zeros_like(diag)] * 2
    for sign, grad, value in (
        (1.0, total, mine),
        (-1.0, gz_own, target[:, :, :, 1:]),
        (-1.0, gy, nxt(mine, -2)),
        (-1.0, gx, nxt(mine, -1)),
    ):
        right = [old + sign * part for old, part in zip(right, herm(grad, value))]
    return jnp.stack(rows + right)


def applied(coefs, field):
    planes, lines = field.shape[1:3]

    def at(array, dz, dy, dx):
        cut = array[..., 1 + dz : planes - 1 + dz, 1 + dy : lines - 1 + dy, :]
        return nxt(cut, -1) if dx == 1 else prv(cut, -1) if dx == -1 else cut

    def mul(c, m, conj):
        re, im = (c[0], -c[1]) if conj else (c[0], c[1])
        return re * m[0] - im * m[1], re * m[1] + im * m[0]

    middle = (coefs[0:1] + DAMPING) * field
    out = [at(middle[0], 0, 0, 0), at(middle[1], 0, 0, 0)]
    unit = ((1, 0, 0), (0, 1, 0), (0, 0, 1))
    for d in range(3):
        e = unit[d]
        pair = coefs[1 + 2 * d : 3 + 2 * d]
        for part in (
            mul(at(pair, 0, 0, 0), at(field, *(-v for v in e)), False),
            mul(at(pair, *e), at(field, *e), True),
        ):
            out = [old + new for old, new in zip(out, part)]
    for k, (d, q) in enumerate(((0, 1), (0, 2), (1, 2))):
        e, h = unit[d], unit[q]
        pair = coefs[7 + 2 * k : 9 + 2 * k]
        diff = tuple(v - w for v, w in zip(e, h))
        for part in (
            mul(at(pair, *e), at(field, *diff), False),
            mul(at(pair, *h), at(field, *(-v for v in diff)), True),
        ):
            out = [old + new for old, new in zip(out, part)]
    return jnp.stack(out)


def body(displacement, freq_index, tissue):
    core = lax.axis_index("freq") % 2
    chips = lax.axis_size("freq") // 2
    low = core == 0
    field = displacement[0]
    weight = tissue.astype(jnp.float32)
    ny, nx = field.shape[-2:]
    kappa = 0.2 * (freq_index[0] + 1).astype(jnp.float32)

    first = jnp.concatenate([field[:, :, 0].reshape(6, ny, nx), weight[0:1]])
    last = jnp.concatenate([field[:, :, 3].reshape(6, ny, nx), weight[3:4]])
    own_edge = to_slabs(jnp.where(low, last, first), 0, 0)
    other_edge = to_slabs(jnp.where(low, first, last), 1, 1)
    sent = jnp.where(low, field[:, :, 1:], field[:, :, :3])
    other_mid = swap_cores(sent)
    other_kappa = swap_cores(kappa.reshape(1, 1))[0, 0]

    bottom = low & (lax.axis_index("gz") == 0)

    def joined(edge, middle):
        edge = jnp.where(bottom, middle[:, :, :1], edge[:6].reshape(2, 3, 1, ny, nx))
        return jnp.where(low, jnp.concatenate([edge, middle], axis=2), jnp.concatenate([middle, edge], axis=2))

    own_mid = jnp.where(low, field[:, :, :3], field[:, :, 1:])
    groups = jnp.stack([joined(own_edge, own_mid), joined(other_edge, other_mid)])
    mask = jnp.where(low, weight[:3], jnp.concatenate([weight[2:], own_edge[6:7]]))
    local = stencil(groups, jnp.stack([kappa, other_kappa]), mask)

    padded = jnp.pad(local, [(0, 0), (0, 0), (2, 2), (0, 0)])
    parts = jnp.stack([padded[:, :, ROWS * j : ROWS * j + ROWS + 4] for j in range(chips)])
    arrived = over_chips(parts.reshape(chips, -1, nx))
    mine = arrived.sum(axis=0).reshape(15, 2, ROWS + 4, nx)

    near = swap_cores(mine)
    far = to_slabs(mine, 1, 1)
    below = jnp.where(low, far, near)
    above = jnp.where(low, near, far)
    block = jnp.concatenate([below, mine, above], axis=1)
    coefs, v0 = block[:13], block[13:]
    v1 = applied(coefs, v0)
    v2 = applied(coefs[:, 1:-1, 1:-1], v1)
    v0, v1 = v0[:, 2:4, 2:-2], v1[:, 1:3, 1:-1]
    moments = [jnp.sum(a * b) for a, b in ((v0, v0), (v0, v1), (v1, v1), (v1, v2))]
    lane = lax.broadcasted_iota(jnp.int32, (ROWS, nx), 1)
    note = sum(jnp.where(lane == k, value, 0.0) for k, value in enumerate(moments))
    tiles = jnp.concatenate([jnp.stack([v0, v1, v2]).reshape(12, ROWS, nx), note[None]])

    gathered = over_chips(jnp.broadcast_to(tiles, (chips, *tiles.shape)))
    others = swap_cores(gathered)
    both = jnp.stack([jnp.where(low, gathered, others), jnp.where(low, others, gathered)])

    sums = both[:, :, 12, 0].sum(axis=(0, 1))
    slabs = lax.axis_size("gz")
    sums = lax.all_to_all(jnp.broadcast_to(sums, (slabs, 1, nx)), "gz", split_axis=0, concat_axis=0, tiled=True)
    sums = sums.sum(axis=(0, 1))
    m0, m1, m2, m3 = (sums[k] for k in range(4))
    step = m0 / m1
    norm = step * step * m2 - m0
    ratio = norm / m0
    grown = 1.0 + ratio
    curve = grown * grown * m1 - 2.0 * step * grown * m2 + step * step * m3
    second = norm / curve
    p, q = step + second * grown, step * second

    vectors = both[:, :, :12].reshape(2, chips, 3, 2, 2, ROWS, nx)
    vectors = vectors.transpose(2, 3, 0, 4, 1, 5, 6).reshape(3, 2, 4, ny, nx)
    modulus = p * vectors[0] - q * vectors[1]
    residual = vectors[0] - p * vectors[1] + q * vectors[2]
    return modulus, residual


def solution(mesh):
    placed = (P("freq", None, None, "gz", None, None), P("freq"), P("gz", None, None))
    return jax.shard_map(
        body,
        mesh=mesh,
        in_specs=placed,
        out_specs=(P(None, "gz", None, None), P(None, "gz", None, None)),
        check_vma=False,
    )
```

```python
import jax
import jax.numpy as jnp
from jax import lax
from jax.sharding import PartitionSpec as P

DAMPING = 0.05
ROWS = 8


def swap_cores(array):
    pairs = [(i, i ^ 1) for i in range(lax.axis_size("freq"))]
    return lax.ppermute(array, "freq", pairs)


def to_slabs(array, first_up, cross):
    peers, slabs = lax.axis_size("freq"), lax.axis_size("gz")
    pairs = []
    for f in range(peers):
        for g in range(slabs):
            to = g + 1 if f % 2 == first_up else g - 1
            if 0 <= to < slabs:
                pairs.append((f * slabs + g, (f ^ cross) * slabs + to))
    return lax.ppermute(array, ("freq", "gz"), pairs)


def over_chips(parts):
    peers = lax.axis_size("freq")
    groups = [list(range(core, peers, 2)) for core in range(2)]
    return lax.all_to_all(parts, "freq", split_axis=0, concat_axis=0, tiled=True, axis_index_groups=groups)


def nxt(field, dim):
    dim = dim % field.ndim
    pad = [(0, 0)] * field.ndim
    pad[dim] = (0, 1)
    return lax.slice_in_dim(jnp.pad(field, pad), 1, field.shape[dim] + 1, axis=dim)


def prv(field, dim):
    dim = dim % field.ndim
    pad = [(0, 0)] * field.ndim
    pad[dim] = (1, 0)
    return lax.slice_in_dim(jnp.pad(field, pad), 0, field.shape[dim], axis=dim)


def herm(a, b):
    real = jnp.sum(a[:, 0] * b[:, 0] + a[:, 1] * b[:, 1], axis=(0, 1))
    imag = jnp.sum(a[:, 0] * b[:, 1] - a[:, 1] * b[:, 0], axis=(0, 1))
    return real, imag


def square(a):
    return jnp.sum(a * a, axis=(0, 1, 2))


def stencil(field, kappa, mask):
    own = field[:, :, :, 1:3]
    gz = field[:, :, :, 1:] - field[:, :, :, :-1]
    gy = nxt(own, -2) - own
    gx = nxt(own, -1) - own
    here = mask[:2]
    gz_own, gz_prv = gz[:, :, :, 1:], gz[:, :, :, :-1]
    total = gz_own + gy + gx
    gy_prv, gx_prv = prv(gy, -2), prv(gx, -1)
    my, mx = nxt(here, -2), nxt(here, -1)
    diag = here * square(total) + mask[1:] * square(gz_own) + my * square(gy) + mx * square(gx)
    rows = [diag]
    for other in (gz_prv, gy_prv, gx_prv):
        rows += [-here * part for part in herm(total, other)]
    for one, two in ((gz_prv, gy_prv), (gz_prv, gx_prv), (gy_prv, gx_prv)):
        rows += [here * part for part in herm(one, two)]
    scaled = -kappa[:, None, None, None, None, None] * field[:, :, :, 1:]
    target = scaled * mask
    mine = target[:, :, :, :2]
    right = [jnp.zeros_like(diag)] * 2
    for sign, grad, value in (
        (1.0, total, mine),
        (-1.0, gz_own, target[:, :, :, 1:]),
        (-1.0, gy, nxt(mine, -2)),
        (-1.0, gx, nxt(mine, -1)),
    ):
        right = [old + sign * part for old, part in zip(right, herm(grad, value))]
    return jnp.stack(rows + right)


def applied(coefs, field):
    planes, lines = field.shape[1:3]

    def at(array, dz, dy, dx):
        cut = array[..., 1 + dz : planes - 1 + dz, 1 + dy : lines - 1 + dy, :]
        return nxt(cut, -1) if dx == 1 else prv(cut, -1) if dx == -1 else cut

    def mul(c, m, conj):
        re, im = (c[0], -c[1]) if conj else (c[0], c[1])
        return re * m[0] - im * m[1], re * m[1] + im * m[0]

    middle = (coefs[0:1] + DAMPING) * field
    out = [at(middle[0], 0, 0, 0), at(middle[1], 0, 0, 0)]
    unit = ((1, 0, 0), (0, 1, 0), (0, 0, 1))
    for d in range(3):
        e = unit[d]
        pair = coefs[1 + 2 * d : 3 + 2 * d]
        for part in (
            mul(at(pair, 0, 0, 0), at(field, *(-v for v in e)), False),
            mul(at(pair, *e), at(field, *e), True),
        ):
            out = [old + new for old, new in zip(out, part)]
    for k, (d, q) in enumerate(((0, 1), (0, 2), (1, 2))):
        e, h = unit[d], unit[q]
        pair = coefs[7 + 2 * k : 9 + 2 * k]
        diff = tuple(v - w for v, w in zip(e, h))
        for part in (
            mul(at(pair, *e), at(field, *diff), False),
            mul(at(pair, *h), at(field, *(-v for v in diff)), True),
        ):
            out = [old + new for old, new in zip(out, part)]
    return jnp.stack(out)


def body(displacement, freq_index, tissue):
    core = lax.axis_index("freq") % 2
    chips = lax.axis_size("freq") // 2
    low = core == 0
    field = displacement[0]
    weight = tissue.astype(jnp.float32)
    ny, nx = field.shape[-2:]
    kappa = 0.2 * (freq_index[0] + 1).astype(jnp.float32)

    first = jnp.concatenate([field[:, :, 0].reshape(6, ny, nx), weight[0:1]])
    last = jnp.concatenate([field[:, :, 3].reshape(6, ny, nx), weight[3:4]])
    own_edge = to_slabs(jnp.where(low, last, first), 0, 0)
    other_edge = to_slabs(jnp.where(low, first, last), 1, 1)
    sent = jnp.where(low, field[:, :, 1:], field[:, :, :3])
    other_mid = swap_cores(sent)
    other_kappa = swap_cores(kappa.reshape(1, 1))[0, 0]

    bottom = low & (lax.axis_index("gz") == 0)

    def joined(edge, middle):
        edge = jnp.where(bottom, middle[:, :, :1], edge[:6].reshape(2, 3, 1, ny, nx))
        return jnp.where(low, jnp.concatenate([edge, middle], axis=2), jnp.concatenate([middle, edge], axis=2))

    own_mid = jnp.where(low, field[:, :, :3], field[:, :, 1:])
    groups = jnp.stack([joined(own_edge, own_mid), joined(other_edge, other_mid)])
    mask = jnp.where(low, weight[:3], jnp.concatenate([weight[2:], own_edge[6:7]]))
    local = stencil(groups, jnp.stack([kappa, other_kappa]), mask)

    padded = jnp.pad(local, [(0, 0), (0, 0), (2, 2), (0, 0)])
    parts = jnp.stack([padded[:, :, ROWS * j : ROWS * j + ROWS + 4] for j in range(chips)])
    arrived = over_chips(parts.reshape(chips, -1, nx))
    mine = arrived.sum(axis=0).reshape(15, 2, ROWS + 4, nx)

    edge = jnp.where(low, mine[:13, 0], mine[:13, 1])
    inner = jnp.where(low, mine[:13, 1], mine[:13, 0])
    steps = jnp.concatenate([mine[1:3, 1], mine[7:11, 1]])
    rights = mine[13:].reshape(4, ROWS + 4, nx)
    near = swap_cores(jnp.concatenate([inner, steps, rights]))
    far = to_slabs(jnp.concatenate([edge, steps, rights]), 1, 1)
    below, above = jnp.where(low, far, near), jnp.where(low, near, far)
    blank = jnp.zeros_like(above[:1])
    beyond = jnp.concatenate([blank, above[13:15], blank, blank, blank, blank, above[15:19], blank, blank])
    coefs = jnp.stack([below[:13], mine[:13, 0], mine[:13, 1], above[:13], beyond], axis=1)
    v0 = jnp.concatenate([below[19:].reshape(2, 2, ROWS + 4, nx), mine[13:], above[19:].reshape(2, 2, ROWS + 4, nx)], axis=1)
    coefs = jnp.concatenate([jnp.zeros_like(coefs[:, :1]), coefs], axis=1)
    v1 = applied(coefs, v0)
    v2 = applied(coefs[:, 1:-1, 1:-1], v1)
    v0, v1 = v0[:, 2:4, 2:-2], v1[:, 1:3, 1:-1]
    moments = [jnp.sum(a * b, axis=(0, 1)) for a, b in ((v0, v0), (v0, v1), (v1, v1), (v1, v2))]
    moments = [jnp.sum(m, axis=0, keepdims=True) for m in moments]
    note = jnp.concatenate(moments + [jnp.zeros((ROWS - 4, nx), jnp.float32)])
    tiles = jnp.concatenate([jnp.stack([v0, v1, v2]).reshape(12, ROWS, nx), note[None]])

    gathered = over_chips(jnp.broadcast_to(tiles, (chips, *tiles.shape)))
    others = swap_cores(gathered)

    sums = (gathered[:, 12] + others[:, 12]).sum(axis=0)
    slabs = lax.axis_size("gz")
    sums = lax.all_to_all(jnp.broadcast_to(sums, (slabs, *sums.shape)), "gz", split_axis=0, concat_axis=0, tiled=True)
    sums = sums.sum(axis=0)
    sums = jnp.broadcast_to(sums.sum(axis=1, keepdims=True), sums.shape)
    m0, m1, m2, m3 = (sums[k] for k in range(4))
    step = m0 / m1
    norm = step * step * m2 - m0
    ratio = norm / m0
    grown = 1.0 + ratio
    curve = grown * grown * m1 - 2.0 * step * grown * m2 + step * step * m3
    second = norm / curve
    p, q = step + second * grown, step * second

    both = jnp.stack([jnp.where(low, gathered, others), jnp.where(low, others, gathered)])
    vectors = both[:, :, :12].reshape(2, chips, 3, 2, 2, ROWS, nx)
    vectors = vectors.transpose(2, 3, 0, 4, 1, 5, 6).reshape(3, 2, 4, ny, nx)
    modulus = p * vectors[0] - q * vectors[1]
    residual = vectors[0] - p * vectors[1] + q * vectors[2]
    return modulus, residual


def solution(mesh):
    placed = (P("freq", None, None, "gz", None, None), P("freq"), P("gz", None, None))
    return jax.shard_map(
        body,
        mesh=mesh,
        in_specs=placed,
        out_specs=(P(None, "gz", None, None), P(None, "gz", None, None)),
        check_vma=False,
    )
```

```python
import functools

import jax
import jax.numpy as jnp
from jax import lax
from jax.experimental import pallas as pl
from jax.experimental.pallas import tpu as pltpu
from jax.sharding import PartitionSpec as P

DAMPING = 0.05
ROWS = 8
VMEM_BYTES = 12 << 20

NAMES = ("zr", "zi", "zyr", "zyi", "zxr", "zxi", "rr", "ri", None, None, None, "d", "yr", "yi", "xr", "xi", "yxr", "yxi", None, None)
MAIN = {name: k for k, name in enumerate(NAMES) if name}
AROUND = {
    8: (("zyr", 0, 1, 2), ("zyi", 3, 1, 2), ("zr", 6, 1, 1)),
    9: (("zi", 0, 1, 1), ("zxr", 2, 1, 1), ("zxi", 4, 1, 1), ("xi", 6, 1, 1)),
    10: (("rr", 0, 2, 2), ("ri", 4, 2, 2)),
    18: (("yr", 0, 1, 2), ("yi", 3, 1, 2), ("d", 6, 1, 1)),
    19: (("yxr", 0, 1, 2), ("yxi", 3, 1, 2), ("xr", 6, 1, 1)),
}
PLANE = len(NAMES)
BEYOND = 11


def swap_cores(array):
    pairs = [(i, i ^ 1) for i in range(lax.axis_size("freq"))]
    return lax.ppermute(array, "freq", pairs)


def to_slabs(array, first_up, cross):
    peers, slabs = lax.axis_size("freq"), lax.axis_size("gz")
    pairs = []
    for f in range(peers):
        for g in range(slabs):
            to = g + 1 if f % 2 == first_up else g - 1
            if 0 <= to < slabs:
                pairs.append((f * slabs + g, (f ^ cross) * slabs + to))
    return lax.ppermute(array, ("freq", "gz"), pairs)


def over_chips(parts):
    peers = lax.axis_size("freq")
    groups = [list(range(core, peers, 2)) for core in range(2)]
    return lax.all_to_all(parts, "freq", split_axis=0, concat_axis=0, tiled=True, axis_index_groups=groups)


def rows_of(shape, dim):
    return lax.broadcasted_iota(jnp.int32, shape, dim)


def nxt(x, dim):
    size = x.shape[dim]
    return jnp.where(rows_of(x.shape, dim) == size - 1, 0.0, pltpu.roll(x, size - 1, dim))


def prv(x, dim):
    return jnp.where(rows_of(x.shape, dim) == 0, 0.0, pltpu.roll(x, 1, dim))


def stencil_kernel(place, kappas, field, tissue, same, cross, mid, out, acc):
    core, bottom = place[0], place[1]
    low, floor = core == 0, place[1] == 1
    ny, nx = field.shape[-2:]
    shape = (ny, nx)

    def cell(group, part, comp, k):
        flat = part * 3 + comp
        if group == 0:
            own, edge = field, same
            if 1 <= k <= 2:
                return own[part, comp, 2 * core + k - 1]
            inside = own[part, comp, 1 if k == 0 else 2]
        else:
            edge = cross
            if 1 <= k <= 2:
                return mid[flat * 3 + core + k - 1]
            inside = mid[flat * 3 + (0 if k == 0 else 2)]
        outside = edge[flat]
        if k == 0:
            outside = jnp.where(floor, cell(group, part, comp, 1), outside)
            return jnp.where(low, outside, inside)
        return jnp.where(low, inside, outside)

    masks = [tissue[2 * core + k].astype(jnp.float32) for k in range(2)]
    masks.append(jnp.where(low, tissue[2].astype(jnp.float32), same[6]))
    other_kappa = mid[18]

    for plane in range(2):
        here, above = masks[plane], masks[plane + 1]
        here_y, here_x = nxt(here, 0), nxt(here, 1)
        for group in range(2):
            kappa = kappas[0] if group == 0 else other_kappa
            scales = [m * kappa for m in (here, above, here_y, here_x)]
            for comp in range(3):
                u, gz, gp, gy, gx, hy, hx, s, t = ([] for _ in range(9))
                for part in range(2):
                    below, mine, up = (cell(group, part, comp, plane + k) for k in range(3))
                    right_y, right_x = nxt(mine, 0), nxt(mine, 1)
                    gz.append(up - mine)
                    gp.append(mine - below)
                    gy.append(right_y - mine)
                    gx.append(right_x - mine)
                    hy.append(prv(gy[-1], 0))
                    hx.append(prv(gx[-1], 1))
                    s.append(gz[-1] + gy[-1] + gx[-1])
                    t.append([mine * scales[0], up * scales[1], right_y * scales[2], right_x * scales[3]])

                def re(a, b):
                    return a[0] * b[0] + a[1] * b[1]

                def im(a, b):
                    return a[0] * b[1] - a[1] * b[0]

                new = [re(s, s), re(gz, gz), re(gy, gy), re(gx, gx)]
                for a, b in ((s, gp), (s, hy), (s, hx), (gp, hy), (gp, hx), (hy, hx)):
                    new += [re(a, b), im(a, b)]
                ts = [[t[0][k], t[1][k]] for k in range(4)]
                for f in (re, im):
                    new.append(f(gz, ts[1]) + f(gy, ts[2]) + f(gx, ts[3]) - f(s, ts[0]))
                first = group == 0 and comp == 0
                for k, value in enumerate(new):
                    acc[k] = value if first else acc[k] + value
        done = {"d": here * acc[0] + above * acc[1] + here_y * acc[2] + here_x * acc[3]}
        for k, name in enumerate(("z", "y", "x", "zy", "zx", "yx")):
            signed = -here if k < 3 else here
            done[name + "r"] = signed * acc[4 + 2 * k]
            done[name + "i"] = signed * acc[5 + 2 * k]
        done["rr"], done["ri"] = acc[16], acc[17]
        row = rows_of(shape, 0)
        lane = row % ROWS
        for name, k in MAIN.items():
            out[:, plane * PLANE + k] = done[name].reshape(ny // ROWS, ROWS, nx)
        for k, parts in AROUND.items():
            tile = jnp.zeros(shape, jnp.float32)
            for name, start, before, after in parts:
                moved = pltpu.roll(done[name], start + before, 0)
                back = pltpu.roll(moved, ny - ROWS, 0)
                moved = jnp.where(row < ROWS, 0.0, moved)
                back = jnp.where(row >= ny - ROWS, 0.0, back)
                tile = jnp.where((lane >= start) & (lane < start + before), moved, tile)
                tile = jnp.where((lane >= start + before) & (lane < start + before + after), back, tile)
            out[:, plane * PLANE + k] = tile.reshape(ny // ROWS, ROWS, nx)


def around_of(name):
    for tile, parts in AROUND.items():
        for other, start, before, after in parts:
            if other == name:
                return tile, start, before, after
    raise KeyError(name)


def vectors_kernel(place, mine, near, far, out):
    low = place[0] == 0
    nx = mine.shape[-1]
    half = rows_of((ROWS, nx), 0)

    def spread(get, name):
        tile, start, before, after = around_of(name)
        main = pltpu.roll(get(MAIN[name]), 4, 0)
        side = get(tile)
        turn = (4 - before - start) % ROWS
        side = pltpu.roll(side, turn, 0) if turn else side
        head = jnp.where(half >= 4, main, jnp.where(half >= 4 - before, side, 0.0))
        tail = jnp.where(half < 4, main, jnp.where(half < 4 + after, side, 0.0))
        return jnp.concatenate([head, tail])

    def below(k):
        return jnp.where(low, far[k], near[k])

    def above(k):
        return jnp.where(low, near[k], far[k])

    sources = {
        -2: lambda k: below(PLANE + k),
        -1: below,
        0: lambda k: mine[0, k],
        1: lambda k: mine[1, k],
        2: above,
        3: lambda k: above(PLANE + k),
    }
    couplings = ("z", "zy", "zx", "y", "x", "yx")
    coefs = {}
    for p in range(-1, 4):
        names = couplings[:3] if p == 3 else couplings
        coefs[p] = {n: (spread(sources[p], n + "r"), spread(sources[p], n + "i")) for n in names}
        if p < 3:
            coefs[p]["d"] = spread(sources[p], "d") + DAMPING
    v0 = {p: (spread(sources[p], "rr"), spread(sources[p], "ri")) for p in range(-2, 4)}

    def mul(c, m):
        return c[0] * m[0] - c[1] * m[1], c[0] * m[1] + c[1] * m[0]

    def conj(c, m):
        return c[0] * m[0] + c[1] * m[1], c[0] * m[1] - c[1] * m[0]

    def plus(*terms):
        return tuple(functools.reduce(lambda a, b: a + b, part) for part in zip(*terms))

    def ahead_y(x):
        return pltpu.roll(x, 2 * ROWS - 1, 0)

    def behind_y(x):
        return pltpu.roll(x, 1, 0)

    def apply(field, planes):
        stepped = {}
        flat = {}
        for p in planes + [planes[-1] + 1]:
            c, m = coefs[p], field[p]
            back = field.get(p - 1)
            my = tuple(behind_y(v) for v in m)
            mx = tuple(prv(v, 1) for v in m)
            stepped[p] = plus(conj(c["z"], m), mul(c["zy"], my), mul(c["zx"], mx))
            if p > planes[-1]:
                continue
            ys = plus(conj(c["y"], m), conj(c["zy"], back), mul(c["yx"], mx))
            xs = plus(conj(c["x"], m), conj(c["zx"], back), conj(c["yx"], my))
            flat[p] = plus(
                tuple(c["d"] * v for v in m),
                mul(c["z"], back),
                mul(c["y"], my),
                mul(c["x"], mx),
                tuple(ahead_y(v) for v in ys),
                tuple(nxt(v, 1) for v in xs),
            )
        return {p: plus(flat[p], stepped[p + 1]) for p in planes}

    v1 = apply(v0, [-1, 0, 1, 2])
    v2 = apply(v1, [0, 1])

    def own(x):
        return jnp.where(half < 4, pltpu.roll(x[:ROWS], 4, 0), pltpu.roll(x[ROWS:], 4, 0))

    held = [[[own(v[p][part]) for p in range(2)] for part in range(2)] for v in (v0, v1, v2)]
    note = jnp.zeros((ROWS, nx), jnp.float32)
    for k, (a, b) in enumerate(((0, 0), (0, 1), (1, 1), (1, 2))):
        total = sum(held[a][part][p] * held[b][part][p] for part in range(2) for p in range(2))
        note = jnp.where(half == k, jnp.sum(total, axis=0, keepdims=True), note)
    tiles = [tile for vector in held for parts in vector for tile in parts] + [note]
    for k, tile in enumerate(tiles):
        for chip in range(out.shape[0]):
            out[chip, k] = tile


def outputs_kernel(place, sums, gathered, others, modulus, residual):
    core = place[0]
    chips = gathered.shape[0]
    total = sums[0]
    for k in range(1, sums.shape[0]):
        total = total + sums[k]
    total = jnp.broadcast_to(jnp.sum(total, axis=1, keepdims=True), total.shape)
    m0, m1, m2, m3 = (total[k : k + 1] for k in range(4))
    step = m0 / m1
    norm = step * step * m2 - m0
    grown = 1.0 + norm / m0
    curve = grown * grown * m1 - 2.0 * step * grown * m2 + step * step * m3
    second = norm / curve
    shape = (chips, ROWS, total.shape[-1])
    p = jnp.broadcast_to((step + second * grown).reshape(1, 1, -1), shape)
    q = jnp.broadcast_to((step * second).reshape(1, 1, -1), shape)
    for source, first in ((gathered, 2 * core), (others, 2 - 2 * core)):
        for part in range(2):
            for plane in range(2):
                v0, v1, v2 = (source[:, 4 * k + 2 * part + plane] for k in range(3))
                flat = (chips * ROWS, shape[-1])
                modulus[part, first + plane] = (p * v0 - q * v1).reshape(flat)
                residual[part, first + plane] = (v0 - p * v1 + q * v2).reshape(flat)


def run(kernel, shapes, place, *arrays, scratch=(), scalars=1):
    vmem = pl.BlockSpec(memory_space=pltpu.VMEM)
    smem = pl.BlockSpec(memory_space=pltpu.SMEM)
    return pl.pallas_call(
        kernel,
        out_shape=shapes,
        in_specs=[smem] * scalars + [vmem] * (len(arrays) + 1 - scalars),
        out_specs=jax.tree.map(lambda _: vmem, shapes),
        scratch_shapes=list(scratch),
        compiler_params=pltpu.CompilerParams(vmem_limit_bytes=VMEM_BYTES),
    )(place, *arrays)


def body(displacement, freq_index, tissue):
    core = lax.axis_index("freq") % 2
    chips = lax.axis_size("freq") // 2
    slabs = lax.axis_size("gz")
    low = core == 0
    field = displacement[0]
    ny, nx = field.shape[-2:]
    tile = (ROWS, nx)
    kappa = 0.2 * (freq_index + 1).astype(jnp.float32)
    place = jnp.stack([core, (low & (lax.axis_index("gz") == 0)).astype(jnp.int32)])

    def shape(*dims):
        return jax.ShapeDtypeStruct(dims, jnp.float32)

    first = jnp.concatenate([field[:, :, 0].reshape(6, ny, nx), tissue[0:1].astype(jnp.float32)])
    last = jnp.concatenate([field[:, :, 3].reshape(6, ny, nx), tissue[3:4].astype(jnp.float32)])
    same = to_slabs(jnp.where(low, last, first), 0, 0)
    cross = to_slabs(jnp.where(low, first, last), 1, 1)
    sent = jnp.where(low, field[:, :, 1:], field[:, :, :3]).reshape(18, ny, nx)
    mid = swap_cores(jnp.concatenate([sent, jnp.broadcast_to(kappa[0], (1, ny, nx))]))

    parts = run(
        stencil_kernel,
        shape(chips, 2 * PLANE, *tile),
        place,
        kappa,
        field,
        tissue,
        same,
        cross,
        mid,
        scratch=[pltpu.VMEM((18, ny, nx), jnp.float32)],
        scalars=2,
    )
    mine = over_chips(parts).sum(axis=0).reshape(2, PLANE, *tile)

    down = jnp.concatenate([mine[0], mine[1, :BEYOND]])
    up = jnp.concatenate([mine[1], mine[0, :BEYOND]])
    near = swap_cores(jnp.where(low, up, down))
    far = to_slabs(jnp.where(low, down, up), 1, 1)
    tiles = run(vectors_kernel, shape(chips, 13, *tile), place, mine, near, far)

    gathered = over_chips(tiles)
    others = swap_cores(gathered)
    sums = (gathered[:, 12] + others[:, 12]).sum(axis=0)
    sums = lax.all_to_all(jnp.broadcast_to(sums, (slabs, *tile)), "gz", split_axis=0, concat_axis=0, tiled=True)
    result = shape(2, 4, ny, nx)
    return tuple(run(outputs_kernel, (result, result), place, sums, gathered, others))


def solution(mesh):
    placed = (P("freq", None, None, "gz", None, None), P("freq"), P("gz", None, None))
    return jax.shard_map(
        body,
        mesh=mesh,
        in_specs=placed,
        out_specs=(P(None, "gz", None, None), P(None, "gz", None, None)),
        check_vma=False,
    )
```

```python
import functools

import jax
import jax.numpy as jnp
from jax import lax
from jax.experimental import pallas as pl
from jax.experimental.pallas import tpu as pltpu
from jax.sharding import PartitionSpec as P

DAMPING = 0.05
ROWS = 8
VMEM_BYTES = 12 << 20

NAMES = ("zr", "zi", "zyr", "zyi", "zxr", "zxi", "rr", "ri", None, None, None, "d", "yr", "yi", "xr", "xi", "yxr", "yxi", None, None)
MAIN = {name: k for k, name in enumerate(NAMES) if name}
AROUND = {
    8: (("zyr", 0, 1, 2), ("zyi", 3, 1, 2), ("zr", 6, 1, 1)),
    9: (("zi", 0, 1, 1), ("zxr", 2, 1, 1), ("zxi", 4, 1, 1), ("xi", 6, 1, 1)),
    10: (("rr", 0, 2, 2), ("ri", 4, 2, 2)),
    18: (("yr", 0, 1, 2), ("yi", 3, 1, 2), ("d", 6, 1, 1)),
    19: (("yxr", 0, 1, 2), ("yxi", 3, 1, 2), ("xr", 6, 1, 1)),
}
PLANE = len(NAMES)
BEYOND = 11


def swap_cores(array):
    pairs = [(i, i ^ 1) for i in range(lax.axis_size("freq"))]
    return lax.ppermute(array, "freq", pairs)


def to_slabs(array, first_up, cross):
    peers, slabs = lax.axis_size("freq"), lax.axis_size("gz")
    pairs = []
    for f in range(peers):
        for g in range(slabs):
            to = g + 1 if f % 2 == first_up else g - 1
            if 0 <= to < slabs:
                pairs.append((f * slabs + g, (f ^ cross) * slabs + to))
    return lax.ppermute(array, ("freq", "gz"), pairs)


def over_chips(parts):
    peers = lax.axis_size("freq")
    groups = [list(range(core, peers, 2)) for core in range(2)]
    return lax.all_to_all(parts, "freq", split_axis=0, concat_axis=0, tiled=True, axis_index_groups=groups)


def rows_of(shape, dim):
    return lax.broadcasted_iota(jnp.int32, shape, dim)


def nxt(x, dim):
    size = x.shape[dim]
    return jnp.where(rows_of(x.shape, dim) == size - 1, 0.0, pltpu.roll(x, size - 1, dim))


def prv(x, dim):
    return jnp.where(rows_of(x.shape, dim) == 0, 0.0, pltpu.roll(x, 1, dim))


def products(cell, kappas, here, above, out, first, acc):
    shape = here.shape
    ny, nx = shape
    here_y, here_x = nxt(here, 0), nxt(here, 1)
    for group in range(2):
        scales = [m * kappas[group] for m in (here, above, here_y, here_x)]
        for comp in range(3):
            gz, gp, gy, gx, hy, hx, s, t = ([] for _ in range(8))
            for part in range(2):
                below, mine, up = cell(group, part, comp)
                right_y, right_x = nxt(mine, 0), nxt(mine, 1)
                gz.append(up - mine)
                gp.append(mine - below)
                gy.append(right_y - mine)
                gx.append(right_x - mine)
                hy.append(prv(gy[-1], 0))
                hx.append(prv(gx[-1], 1))
                s.append(gz[-1] + gy[-1] + gx[-1])
                t.append([mine * scales[0], up * scales[1], right_y * scales[2], right_x * scales[3]])

            def re(a, b):
                return a[0] * b[0] + a[1] * b[1]

            def im(a, b):
                return a[0] * b[1] - a[1] * b[0]

            new = [re(s, s), re(gz, gz), re(gy, gy), re(gx, gx)]
            for a, b in ((s, gp), (s, hy), (s, hx), (gp, hy), (gp, hx), (hy, hx)):
                new += [re(a, b), im(a, b)]
            ts = [[t[0][k], t[1][k]] for k in range(4)]
            for f in (re, im):
                new.append(f(gz, ts[1]) + f(gy, ts[2]) + f(gx, ts[3]) - f(s, ts[0]))
            for k, value in enumerate(new):
                acc[k] = value if group == 0 and comp == 0 else acc[k] + value
    done = {"d": here * acc[0] + above * acc[1] + here_y * acc[2] + here_x * acc[3]}
    for k, name in enumerate(("z", "y", "x", "zy", "zx", "yx")):
        signed = -here if k < 3 else here
        done[name + "r"] = signed * acc[4 + 2 * k]
        done[name + "i"] = signed * acc[5 + 2 * k]
    done["rr"], done["ri"] = acc[16], acc[17]
    row = rows_of(shape, 0)
    lane = row % ROWS
    for name, k in MAIN.items():
        out[:, first + k] = done[name].reshape(ny // ROWS, ROWS, nx)
    for k, parts in AROUND.items():
        tile = jnp.zeros(shape, jnp.float32)
        for name, start, before, after in parts:
            moved = pltpu.roll(done[name], start + before, 0)
            back = pltpu.roll(moved, ny - ROWS, 0)
            moved = jnp.where(row < ROWS, 0.0, moved)
            back = jnp.where(row >= ny - ROWS, 0.0, back)
            tile = jnp.where((lane >= start) & (lane < start + before), moved, tile)
            tile = jnp.where((lane >= start + before) & (lane < start + before + after), back, tile)
        out[:, first + k] = tile.reshape(ny // ROWS, ROWS, nx)


def kappa_of(index):
    return 0.2 * (index[0] + 1).astype(jnp.float32)


def inner_kernel(place, index, other_index, field, other, tissue, out, acc):
    core = place[0]

    def cell(group, part, comp):
        source = field if group == 0 else other
        return [source[part, comp, core + k] for k in range(3)]

    here, above = (tissue[core + k].astype(jnp.float32) for k in (1, 2))
    products(cell, (kappa_of(index), kappa_of(other_index)), here, above, out, 0, acc)


def outer_kernel(place, index, other_index, field, other, tissue, edge, _, out, acc):
    core = place[0]
    low, floor = core == 0, place[1] == 1

    def cell(group, part, comp):
        source = field if group == 0 else other
        outside = edge[6 * (1 - group) + 3 * part + comp]
        mine, inside = source[part, comp, 3 * core], source[part, comp, 1 + core]
        below = jnp.where(low, jnp.where(floor, mine, outside), inside)
        return below, mine, jnp.where(low, inside, outside)

    here = tissue[3 * core].astype(jnp.float32)
    above = jnp.where(low, tissue[1].astype(jnp.float32), edge[12])
    products(cell, (kappa_of(index), kappa_of(other_index)), here, above, out, PLANE, acc)


def around_of(name):
    for tile, parts in AROUND.items():
        for other, start, before, after in parts:
            if other == name:
                return tile, start, before, after
    raise KeyError(name)


def vectors_kernel(place, mine, near, far, out):
    core = place[0]
    low = core == 0
    nx = mine.shape[-1]
    half = rows_of((ROWS, nx), 0)

    def spread(get, name):
        tile, start, before, after = around_of(name)
        main = pltpu.roll(get(MAIN[name]), 4, 0)
        side = get(tile)
        turn = (4 - before - start) % ROWS
        side = pltpu.roll(side, turn, 0) if turn else side
        head = jnp.where(half >= 4, main, jnp.where(half >= 4 - before, side, 0.0))
        tail = jnp.where(half < 4, main, jnp.where(half < 4 + after, side, 0.0))
        return jnp.concatenate([head, tail])

    def below(k):
        return jnp.where(low, far[k], near[k])

    def above(k):
        return jnp.where(low, near[k], far[k])

    sources = {
        -2: lambda k: below(PLANE + k),
        -1: below,
        0: lambda k: mine[1 - core, k],
        1: lambda k: mine[core, k],
        2: above,
        3: lambda k: above(PLANE + k),
    }
    couplings = ("z", "zy", "zx", "y", "x", "yx")
    coefs = {}
    for p in range(-1, 4):
        names = couplings[:3] if p == 3 else couplings
        coefs[p] = {n: (spread(sources[p], n + "r"), spread(sources[p], n + "i")) for n in names}
        if p < 3:
            coefs[p]["d"] = spread(sources[p], "d") + DAMPING
    v0 = {p: (spread(sources[p], "rr"), spread(sources[p], "ri")) for p in range(-2, 4)}

    def mul(c, m):
        return c[0] * m[0] - c[1] * m[1], c[0] * m[1] + c[1] * m[0]

    def conj(c, m):
        return c[0] * m[0] + c[1] * m[1], c[0] * m[1] - c[1] * m[0]

    def plus(*terms):
        return tuple(functools.reduce(lambda a, b: a + b, part) for part in zip(*terms))

    def ahead_y(x):
        return pltpu.roll(x, 2 * ROWS - 1, 0)

    def behind_y(x):
        return pltpu.roll(x, 1, 0)

    def apply(field, planes):
        stepped = {}
        flat = {}
        for p in planes + [planes[-1] + 1]:
            c, m = coefs[p], field[p]
            back = field.get(p - 1)
            my = tuple(behind_y(v) for v in m)
            mx = tuple(prv(v, 1) for v in m)
            stepped[p] = plus(conj(c["z"], m), mul(c["zy"], my), mul(c["zx"], mx))
            if p > planes[-1]:
                continue
            ys = plus(conj(c["y"], m), conj(c["zy"], back), mul(c["yx"], mx))
            xs = plus(conj(c["x"], m), conj(c["zx"], back), conj(c["yx"], my))
            flat[p] = plus(
                tuple(c["d"] * v for v in m),
                mul(c["z"], back),
                mul(c["y"], my),
                mul(c["x"], mx),
                tuple(ahead_y(v) for v in ys),
                tuple(nxt(v, 1) for v in xs),
            )
        return {p: plus(flat[p], stepped[p + 1]) for p in planes}

    v1 = apply(v0, [-1, 0, 1, 2])
    v2 = apply(v1, [0, 1])

    def own(x):
        return jnp.where(half < 4, pltpu.roll(x[:ROWS], 4, 0), pltpu.roll(x[ROWS:], 4, 0))

    held = [[[own(v[p][part]) for p in range(2)] for part in range(2)] for v in (v0, v1, v2)]
    note = jnp.zeros((ROWS, nx), jnp.float32)
    for k, (a, b) in enumerate(((0, 0), (0, 1), (1, 1), (1, 2))):
        total = sum(held[a][part][p] * held[b][part][p] for part in range(2) for p in range(2))
        note = jnp.where(half == k, jnp.sum(total, axis=0, keepdims=True), note)
    tiles = [tile for vector in held for parts in vector for tile in parts] + [note]
    for k, tile in enumerate(tiles):
        for chip in range(out.shape[0]):
            out[chip, k] = tile


def outputs_kernel(place, sums, gathered, others, modulus, residual):
    core = place[0]
    chips = gathered.shape[0]
    total = sums[0]
    for k in range(1, sums.shape[0]):
        total = total + sums[k]
    total = jnp.broadcast_to(jnp.sum(total, axis=1, keepdims=True), total.shape)
    m0, m1, m2, m3 = (total[k : k + 1] for k in range(4))
    step = m0 / m1
    norm = step * step * m2 - m0
    grown = 1.0 + norm / m0
    curve = grown * grown * m1 - 2.0 * step * grown * m2 + step * step * m3
    second = norm / curve
    shape = (chips, ROWS, total.shape[-1])
    p = jnp.broadcast_to((step + second * grown).reshape(1, 1, -1), shape)
    q = jnp.broadcast_to((step * second).reshape(1, 1, -1), shape)
    for source, first in ((gathered, 2 * core), (others, 2 - 2 * core)):
        for part in range(2):
            for plane in range(2):
                v0, v1, v2 = (source[:, 4 * k + 2 * part + plane] for k in range(3))
                flat = (chips * ROWS, shape[-1])
                modulus[part, first + plane] = (p * v0 - q * v1).reshape(flat)
                residual[part, first + plane] = (v0 - p * v1 + q * v2).reshape(flat)


def run(kernel, shapes, *arrays, scratch=(), scalars=1, aliases=None):
    vmem = pl.BlockSpec(memory_space=pltpu.VMEM)
    smem = pl.BlockSpec(memory_space=pltpu.SMEM)
    return pl.pallas_call(
        kernel,
        out_shape=shapes,
        in_specs=[smem] * scalars + [vmem] * (len(arrays) - scalars),
        out_specs=jax.tree.map(lambda _: vmem, shapes),
        scratch_shapes=list(scratch),
        input_output_aliases=aliases or {},
        compiler_params=pltpu.CompilerParams(vmem_limit_bytes=VMEM_BYTES),
    )(*arrays)


def body(displacement, freq_index, tissue):
    core = lax.axis_index("freq") % 2
    chips = lax.axis_size("freq") // 2
    slabs = lax.axis_size("gz")
    low = core == 0
    ny, nx = displacement.shape[-2:]
    tile = (ROWS, nx)
    place = jnp.stack([core, (low & (lax.axis_index("gz") == 0)).astype(jnp.int32)])

    def shape(*dims):
        return jax.ShapeDtypeStruct(dims, jnp.float32)

    other = swap_cores(displacement)[0]
    other_index = swap_cores(freq_index)
    field = displacement[0]

    def plane(array, k):
        return array[:, :, k].reshape(6, ny, nx)

    first, last = (
        jnp.concatenate([plane(field, k), plane(other, k), tissue[k : k + 1].astype(jnp.float32)]) for k in (0, 3)
    )
    edge = to_slabs(jnp.where(low, first, last), 1, 1)

    held = (place, freq_index, other_index, field, other, tissue)
    scratch = [pltpu.VMEM((18, ny, nx), jnp.float32)]
    message = shape(chips, 2 * PLANE, *tile)
    parts = run(inner_kernel, message, *held, scratch=scratch, scalars=3)
    parts = run(outer_kernel, message, *held, edge, parts, scratch=scratch, scalars=3, aliases={7: 0})
    mine = over_chips(parts).sum(axis=0).reshape(2, PLANE, *tile)

    near = swap_cores(jnp.concatenate([mine[0], mine[1, :BEYOND]]))
    far = to_slabs(jnp.concatenate([mine[1], mine[0, :BEYOND]]), 1, 1)
    tiles = run(vectors_kernel, shape(chips, 13, *tile), place, mine, near, far)

    gathered = over_chips(tiles)
    others = swap_cores(gathered)
    sums = (gathered[:, 12] + others[:, 12]).sum(axis=0)
    sums = lax.all_to_all(jnp.broadcast_to(sums, (slabs, *tile)), "gz", split_axis=0, concat_axis=0, tiled=True)
    result = shape(2, 4, ny, nx)
    return tuple(run(outputs_kernel, (result, result), place, sums, gathered, others))


def solution(mesh):
    placed = (P("freq", None, None, "gz", None, None), P("freq"), P("gz", None, None))
    return jax.shard_map(
        body,
        mesh=mesh,
        in_specs=placed,
        out_specs=(P(None, "gz", None, None), P(None, "gz", None, None)),
        check_vma=False,
    )
```

```python
import functools

import jax
import jax.numpy as jnp
from jax import lax
from jax.experimental import pallas as pl
from jax.experimental.pallas import tpu as pltpu
from jax.sharding import PartitionSpec as P

DAMPING = 0.05
ROWS = 8
VMEM_BYTES = 12 << 20

NAMES = ("zr", "zi", "zyr", "zyi", "zxr", "zxi", "rr", "ri", None, None, None, "d", "yr", "yi", "xr", "xi", "yxr", "yxi", None, None)
MAIN = {name: k for k, name in enumerate(NAMES) if name}
AROUND = {
    8: (("zyr", 0, 1, 2), ("zyi", 3, 1, 2), ("zr", 6, 1, 1)),
    9: (("zi", 0, 1, 1), ("zxr", 2, 1, 1), ("zxi", 4, 1, 1), ("xi", 6, 1, 1)),
    10: (("rr", 0, 2, 2), ("ri", 4, 2, 2)),
    18: (("yr", 0, 1, 2), ("yi", 3, 1, 2), ("d", 6, 1, 1)),
    19: (("yxr", 0, 1, 2), ("yxi", 3, 1, 2), ("xr", 6, 1, 1)),
}
PLANE = len(NAMES)
BEYOND = 11


def swap_cores(array):
    pairs = [(i, i ^ 1) for i in range(lax.axis_size("freq"))]
    return lax.ppermute(array, "freq", pairs)


def to_slabs(array, first_up, cross):
    peers, slabs = lax.axis_size("freq"), lax.axis_size("gz")
    pairs = []
    for f in range(peers):
        for g in range(slabs):
            to = g + 1 if f % 2 == first_up else g - 1
            if 0 <= to < slabs:
                pairs.append((f * slabs + g, (f ^ cross) * slabs + to))
    return lax.ppermute(array, ("freq", "gz"), pairs)


def over_chips(parts):
    peers = lax.axis_size("freq")
    groups = [list(range(core, peers, 2)) for core in range(2)]
    return lax.all_to_all(parts, "freq", split_axis=0, concat_axis=0, tiled=True, axis_index_groups=groups)


def rows_of(shape, dim):
    return lax.broadcasted_iota(jnp.int32, shape, dim)


def nxt(x, dim):
    size = x.shape[dim]
    return jnp.where(rows_of(x.shape, dim) == size - 1, 0.0, pltpu.roll(x, size - 1, dim))


def prv(x, dim):
    return jnp.where(rows_of(x.shape, dim) == 0, 0.0, pltpu.roll(x, 1, dim))


def products(cell, kappas, masks, out, first, rows):
    nx = out.shape[-1]
    ny = out.shape[0] * ROWS
    tile = (ROWS, nx)
    line, lane = rows_of(tile, 0), rows_of(tile, 1)
    blank = jnp.zeros(tile, jnp.float32)

    def at(read, j):
        return read(pl.ds(ROWS * j, ROWS))

    def next_y(read, j):
        if ROWS * j + ROWS < ny:
            return read(pl.ds(ROWS * j + 1, ROWS))
        return jnp.where(line == ROWS - 1, 0.0, pltpu.roll(at(read, j), ROWS - 1, 0))

    def prev_y(read, j):
        if j:
            return read(pl.ds(ROWS * j - 1, ROWS))
        return pltpu.roll(at(read, j), 1, 0)

    def re(a, b):
        return a[0] * b[0] + a[1] * b[1]

    def im(a, b):
        return a[0] * b[1] - a[1] * b[0]

    names = [name for name in NAMES if name]
    for k in range(len(names)):
        rows[k, :ROWS] = blank
        rows[k, ROWS + ny :] = blank
    for j in range(ny // ROWS):
        here, above = (at(mask, j) for mask in masks)
        here_y, here_x = next_y(masks[0], j), nxt(here, 1)
        sums = None
        for group in range(2):
            scales = [m * kappas[group] for m in (here, above, here_y, here_x)]
            for comp in range(3):
                gz, gp, gy, gx, hy, hx, s, t = ([] for _ in range(8))
                for part in range(2):
                    below, mine, up = cell(group, part, comp)
                    u, uz = at(mine, j), at(up, j)
                    uy, ux = next_y(mine, j), nxt(u, 1)
                    gz.append(uz - u)
                    gp.append(u - at(below, j))
                    gy.append(uy - u)
                    gx.append(ux - u)
                    step = u - prev_y(mine, j)
                    hy.append(step if j else jnp.where(line == 0, 0.0, step))
                    hx.append(jnp.where(lane == 0, 0.0, u - pltpu.roll(u, 1, 1)))
                    s.append(gz[-1] + gy[-1] + gx[-1])
                    t.append([u * scales[0], uz * scales[1], uy * scales[2], ux * scales[3]])
                new = [re(s, s), re(gz, gz), re(gy, gy), re(gx, gx)]
                for a, b in ((s, gp), (s, hy), (s, hx), (gp, hy), (gp, hx), (hy, hx)):
                    new += [re(a, b), im(a, b)]
                ts = [[t[0][k], t[1][k]] for k in range(4)]
                for f in (re, im):
                    new.append(f(gz, ts[1]) + f(gy, ts[2]) + f(gx, ts[3]) - f(s, ts[0]))
                sums = new if sums is None else [old + value for old, value in zip(sums, new)]
        done = {"d": here * sums[0] + above * sums[1] + here_y * sums[2] + here_x * sums[3]}
        for k, name in enumerate(("z", "y", "x", "zy", "zx", "yx")):
            signed = -here if k < 3 else here
            done[name + "r"] = signed * sums[4 + 2 * k]
            done[name + "i"] = signed * sums[5 + 2 * k]
        done["rr"], done["ri"] = sums[16], sums[17]
        for k, name in enumerate(names):
            out[j, first + MAIN[name]] = done[name]
            rows[k, ROWS + ROWS * j : 2 * ROWS + ROWS * j] = done[name]
    for j in range(ny // ROWS):
        for k, parts in AROUND.items():
            packed = blank
            for name, start, before, after in parts:
                kept = names.index(name)
                middle = start + before
                head = rows[kept, pl.ds(ROWS + ROWS * j - middle, ROWS)]
                tail = rows[kept, pl.ds(2 * ROWS + ROWS * j - middle, ROWS)]
                packed = jnp.where((line >= start) & (line < middle), head, packed)
                packed = jnp.where((line >= middle) & (line < middle + after), tail, packed)
            out[j, first + k] = packed


def kappa_of(index):
    return 0.2 * (index[0] + 1).astype(jnp.float32)


def inner_kernel(place, index, other_index, field, other, tissue, out, rows):
    core = place[0]

    def cell(group, part, comp):
        source = field if group == 0 else other
        return [lambda at, k=k: source[part, comp, core + k, at] for k in range(3)]

    masks = [lambda at, k=k: tissue[core + k, at].astype(jnp.float32) for k in (1, 2)]
    products(cell, (kappa_of(index), kappa_of(other_index)), masks, out, 0, rows)


def outer_kernel(place, index, other_index, field, other, tissue, edge, inner, out, rows):
    core = place[0]
    low, floor = core == 0, place[1] == 1
    out[:, :PLANE] = inner[...]

    def cell(group, part, comp):
        source = field if group == 0 else other

        def outside(at):
            return edge[6 * (1 - group) + 3 * part + comp, at]

        def mine(at):
            return source[part, comp, 3 * core, at]

        def inside(at):
            return source[part, comp, 1 + core, at]

        def below(at):
            return jnp.where(low, jnp.where(floor, mine(at), outside(at)), inside(at))

        return below, mine, lambda at: jnp.where(low, inside(at), outside(at))

    def here(at):
        return tissue[3 * core, at].astype(jnp.float32)

    def above(at):
        return jnp.where(low, tissue[1, at].astype(jnp.float32), edge[12, at])

    products(cell, (kappa_of(index), kappa_of(other_index)), (here, above), out, PLANE, rows)


def around_of(name):
    for tile, parts in AROUND.items():
        for other, start, before, after in parts:
            if other == name:
                return tile, start, before, after
    raise KeyError(name)


def vectors_kernel(place, mine, near, far, out):
    core = place[0]
    low = core == 0
    nx = mine.shape[-1]
    half = rows_of((ROWS, nx), 0)

    def spread(get, name):
        tile, start, before, after = around_of(name)
        main = pltpu.roll(get(MAIN[name]), 4, 0)
        side = get(tile)
        turn = (4 - before - start) % ROWS
        side = pltpu.roll(side, turn, 0) if turn else side
        head = jnp.where(half >= 4, main, jnp.where(half >= 4 - before, side, 0.0))
        tail = jnp.where(half < 4, main, jnp.where(half < 4 + after, side, 0.0))
        return jnp.concatenate([head, tail])

    def below(k):
        return jnp.where(low, far[k], near[k])

    def above(k):
        return jnp.where(low, near[k], far[k])

    sources = {
        -2: lambda k: below(PLANE + k),
        -1: below,
        0: lambda k: mine[1 - core, k],
        1: lambda k: mine[core, k],
        2: above,
        3: lambda k: above(PLANE + k),
    }
    couplings = ("z", "zy", "zx", "y", "x", "yx")
    coefs = {}
    for p in range(-1, 4):
        names = couplings[:3] if p == 3 else couplings
        coefs[p] = {n: (spread(sources[p], n + "r"), spread(sources[p], n + "i")) for n in names}
        if p < 3:
            coefs[p]["d"] = spread(sources[p], "d") + DAMPING
    v0 = {p: (spread(sources[p], "rr"), spread(sources[p], "ri")) for p in range(-2, 4)}

    def mul(c, m):
        return c[0] * m[0] - c[1] * m[1], c[0] * m[1] + c[1] * m[0]

    def conj(c, m):
        return c[0] * m[0] + c[1] * m[1], c[0] * m[1] - c[1] * m[0]

    def plus(*terms):
        return tuple(functools.reduce(lambda a, b: a + b, part) for part in zip(*terms))

    def ahead_y(x):
        return pltpu.roll(x, 2 * ROWS - 1, 0)

    def behind_y(x):
        return pltpu.roll(x, 1, 0)

    def apply(field, planes):
        stepped = {}
        flat = {}
        for p in planes + [planes[-1] + 1]:
            c, m = coefs[p], field[p]
            back = field.get(p - 1)
            my = tuple(behind_y(v) for v in m)
            mx = tuple(prv(v, 1) for v in m)
            stepped[p] = plus(conj(c["z"], m), mul(c["zy"], my), mul(c["zx"], mx))
            if p > planes[-1]:
                continue
            ys = plus(conj(c["y"], m), conj(c["zy"], back), mul(c["yx"], mx))
            xs = plus(conj(c["x"], m), conj(c["zx"], back), conj(c["yx"], my))
            flat[p] = plus(
                tuple(c["d"] * v for v in m),
                mul(c["z"], back),
                mul(c["y"], my),
                mul(c["x"], mx),
                tuple(ahead_y(v) for v in ys),
                tuple(nxt(v, 1) for v in xs),
            )
        return {p: plus(flat[p], stepped[p + 1]) for p in planes}

    v1 = apply(v0, [-1, 0, 1, 2])
    v2 = apply(v1, [0, 1])

    def own(x):
        return jnp.where(half < 4, pltpu.roll(x[:ROWS], 4, 0), pltpu.roll(x[ROWS:], 4, 0))

    held = [[[own(v[p][part]) for p in range(2)] for part in range(2)] for v in (v0, v1, v2)]
    note = jnp.zeros((ROWS, nx), jnp.float32)
    for k, (a, b) in enumerate(((0, 0), (0, 1), (1, 1), (1, 2))):
        total = sum(held[a][part][p] * held[b][part][p] for part in range(2) for p in range(2))
        note = jnp.where(half == k, jnp.sum(total, axis=0, keepdims=True), note)
    tiles = [tile for vector in held for parts in vector for tile in parts] + [note]
    for k, tile in enumerate(tiles):
        for chip in range(out.shape[0]):
            out[chip, k] = tile


def outputs_kernel(place, sums, gathered, others, modulus, residual):
    core = place[0]
    chips = gathered.shape[0]
    total = sums[0]
    for k in range(1, sums.shape[0]):
        total = total + sums[k]
    total = jnp.broadcast_to(jnp.sum(total, axis=1, keepdims=True), total.shape)
    m0, m1, m2, m3 = (total[k : k + 1] for k in range(4))
    step = m0 / m1
    norm = step * step * m2 - m0
    grown = 1.0 + norm / m0
    curve = grown * grown * m1 - 2.0 * step * grown * m2 + step * step * m3
    second = norm / curve
    shape = (chips, ROWS, total.shape[-1])
    p = jnp.broadcast_to((step + second * grown).reshape(1, 1, -1), shape)
    q = jnp.broadcast_to((step * second).reshape(1, 1, -1), shape)
    for source, first in ((gathered, 2 * core), (others, 2 - 2 * core)):
        for part in range(2):
            for plane in range(2):
                v0, v1, v2 = (source[:, 4 * k + 2 * part + plane] for k in range(3))
                flat = (chips * ROWS, shape[-1])
                modulus[part, first + plane] = (p * v0 - q * v1).reshape(flat)
                residual[part, first + plane] = (v0 - p * v1 + q * v2).reshape(flat)


def run(kernel, shapes, *arrays, scratch=(), scalars=1):
    vmem = pl.BlockSpec(memory_space=pltpu.VMEM)
    smem = pl.BlockSpec(memory_space=pltpu.SMEM)
    return pl.pallas_call(
        kernel,
        out_shape=shapes,
        in_specs=[smem] * scalars + [vmem] * (len(arrays) - scalars),
        out_specs=jax.tree.map(lambda _: vmem, shapes),
        scratch_shapes=list(scratch),
        compiler_params=pltpu.CompilerParams(vmem_limit_bytes=VMEM_BYTES),
    )(*arrays)


def body(displacement, freq_index, tissue):
    core = lax.axis_index("freq") % 2
    chips = lax.axis_size("freq") // 2
    slabs = lax.axis_size("gz")
    low = core == 0
    ny, nx = displacement.shape[-2:]
    tile = (ROWS, nx)
    place = jnp.stack([core, (low & (lax.axis_index("gz") == 0)).astype(jnp.int32)])

    def shape(*dims):
        return jax.ShapeDtypeStruct(dims, jnp.float32)

    other = swap_cores(displacement)[0]
    other_index = swap_cores(freq_index)
    field = displacement[0]

    def plane(array, k):
        return array[:, :, k].reshape(6, ny, nx)

    first, last = (
        jnp.concatenate([plane(field, k), plane(other, k), tissue[k : k + 1].astype(jnp.float32)]) for k in (0, 3)
    )
    edge = to_slabs(jnp.where(low, first, last), 1, 1)

    held = (place, freq_index, other_index, field, other, tissue)
    scratch = [pltpu.VMEM((15, ny + 2 * ROWS, nx), jnp.float32)]
    inner = run(inner_kernel, shape(chips, PLANE, *tile), *held, scratch=scratch, scalars=3)
    parts = run(outer_kernel, shape(chips, 2 * PLANE, *tile), *held, edge, inner, scratch=scratch, scalars=3)
    mine = over_chips(parts).sum(axis=0).reshape(2, PLANE, *tile)

    near = swap_cores(jnp.concatenate([mine[0], mine[1, :BEYOND]]))
    far = to_slabs(jnp.concatenate([mine[1], mine[0, :BEYOND]]), 1, 1)
    tiles = run(vectors_kernel, shape(chips, 13, *tile), place, mine, near, far)

    gathered = over_chips(tiles)
    others = swap_cores(gathered)
    sums = gathered[:, 12].sum(axis=0)
    sums = sums + swap_cores(sums)
    sums = lax.all_to_all(jnp.broadcast_to(sums, (slabs, *tile)), "gz", split_axis=0, concat_axis=0, tiled=True)
    result = shape(2, 4, ny, nx)
    return tuple(run(outputs_kernel, (result, result), place, sums, gathered, others))


def solution(mesh):
    placed = (P("freq", None, None, "gz", None, None), P("freq"), P("gz", None, None))
    return jax.shard_map(
        body,
        mesh=mesh,
        in_specs=placed,
        out_specs=(P(None, "gz", None, None), P(None, "gz", None, None)),
        check_vma=False,
    )
```

```python
import functools

import jax
import jax.numpy as jnp
from jax import lax
from jax.experimental import pallas as pl
from jax.experimental.pallas import tpu as pltpu
from jax.sharding import PartitionSpec as P

DAMPING = 0.05
ROWS = 8
VMEM_BYTES = 12 << 20

NAMES = ("zr", "zi", "zyr", "zyi", "zxr", "zxi", "rr", "ri", None, None, None, "d", "yr", "yi", "xr", "xi", "yxr", "yxi", None, None)
MAIN = {name: k for k, name in enumerate(NAMES) if name}
AROUND = {
    8: (("zyr", 0, 1, 2), ("zyi", 3, 1, 2), ("zr", 6, 1, 1)),
    9: (("zi", 0, 1, 1), ("zxr", 2, 1, 1), ("zxi", 4, 1, 1), ("xi", 6, 1, 1)),
    10: (("rr", 0, 2, 2), ("ri", 4, 2, 2)),
    18: (("yr", 0, 1, 2), ("yi", 3, 1, 2), ("d", 6, 1, 1)),
    19: (("yxr", 0, 1, 2), ("yxi", 3, 1, 2), ("xr", 6, 1, 1)),
}
PLANE = len(NAMES)
BEYOND = 11


def swap_cores(array):
    pairs = [(i, i ^ 1) for i in range(lax.axis_size("freq"))]
    return lax.ppermute(array, "freq", pairs)


def to_slabs(array, first_up, cross):
    peers, slabs = lax.axis_size("freq"), lax.axis_size("gz")
    pairs = []
    for f in range(peers):
        for g in range(slabs):
            to = g + 1 if f % 2 == first_up else g - 1
            if 0 <= to < slabs:
                pairs.append((f * slabs + g, (f ^ cross) * slabs + to))
    return lax.ppermute(array, ("freq", "gz"), pairs)


def over_chips(parts):
    peers = lax.axis_size("freq")
    groups = [list(range(core, peers, 2)) for core in range(2)]
    return lax.all_to_all(parts, "freq", split_axis=0, concat_axis=0, tiled=True, axis_index_groups=groups)


def rows_of(shape, dim):
    return lax.broadcasted_iota(jnp.int32, shape, dim)


def nxt(x, dim):
    size = x.shape[dim]
    return jnp.where(rows_of(x.shape, dim) == size - 1, 0.0, pltpu.roll(x, size - 1, dim))


def prv(x, dim):
    return jnp.where(rows_of(x.shape, dim) == 0, 0.0, pltpu.roll(x, 1, dim))


def products(cell, kappas, masks, out, first, rows):
    nx = out.shape[-1]
    ny = out.shape[0] * ROWS
    tile = (ROWS, nx)
    line, lane = rows_of(tile, 0), rows_of(tile, 1)
    blank = jnp.zeros(tile, jnp.float32)

    last = ny // ROWS - 1

    def at(read, j):
        return read(pl.ds(pl.multiple_of(ROWS * j, ROWS), ROWS))

    def next_y(read, j, own):
        after = jnp.where(j == last, 0.0, at(read, jnp.minimum(j + 1, last)))
        return pltpu.roll(jnp.where(line == 0, after, own), ROWS - 1, 0)

    def prev_y(read, j, own):
        before = at(read, jnp.maximum(j - 1, 0))
        return pltpu.roll(jnp.where(line == ROWS - 1, before, own), 1, 0)

    def re(a, b):
        return a[0] * b[0] + a[1] * b[1]

    def im(a, b):
        return a[0] * b[1] - a[1] * b[0]

    names = [name for name in NAMES if name]
    for k in range(len(names)):
        rows[k, :ROWS] = blank
        rows[k, ROWS + ny :] = blank
    def chunk(j, _):
        here, above = (at(mask, j) for mask in masks)
        here_y, here_x = next_y(masks[0], j, here), nxt(here, 1)
        bottom = (line == 0) & (j == 0)
        sums = None
        for group in range(2):
            scales = [m * kappas[group] for m in (here, above, here_y, here_x)]
            for comp in range(3):
                gz, gp, gy, gx, hy, hx, s, t = ([] for _ in range(8))
                for part in range(2):
                    below, mine, up = cell(group, part, comp)
                    u, uz = at(mine, j), at(up, j)
                    uy, ux = next_y(mine, j, u), nxt(u, 1)
                    gz.append(uz - u)
                    gp.append(u - at(below, j))
                    gy.append(uy - u)
                    gx.append(ux - u)
                    hy.append(jnp.where(bottom, 0.0, u - prev_y(mine, j, u)))
                    hx.append(jnp.where(lane == 0, 0.0, u - pltpu.roll(u, 1, 1)))
                    s.append(gz[-1] + gy[-1] + gx[-1])
                    t.append([u * scales[0], uz * scales[1], uy * scales[2], ux * scales[3]])
                new = [re(s, s), re(gz, gz), re(gy, gy), re(gx, gx)]
                for a, b in ((s, gp), (s, hy), (s, hx), (gp, hy), (gp, hx), (hy, hx)):
                    new += [re(a, b), im(a, b)]
                ts = [[t[0][k], t[1][k]] for k in range(4)]
                for f in (re, im):
                    new.append(f(gz, ts[1]) + f(gy, ts[2]) + f(gx, ts[3]) - f(s, ts[0]))
                sums = new if sums is None else [old + value for old, value in zip(sums, new)]
        done = {"d": here * sums[0] + above * sums[1] + here_y * sums[2] + here_x * sums[3]}
        for k, name in enumerate(("z", "y", "x", "zy", "zx", "yx")):
            signed = -here if k < 3 else here
            done[name + "r"] = signed * sums[4 + 2 * k]
            done[name + "i"] = signed * sums[5 + 2 * k]
        done["rr"], done["ri"] = sums[16], sums[17]
        for k, name in enumerate(names):
            out[j, first + MAIN[name]] = done[name]
            rows[k, pl.ds(pl.multiple_of(ROWS * j + ROWS, ROWS), ROWS)] = done[name]
        return 0

    lax.fori_loop(0, ny // ROWS, chunk, 0)

    def surround(j, _):
        def tile_of(name, k):
            return rows[names.index(name), pl.ds(pl.multiple_of(ROWS * (j + k), ROWS), ROWS)]

        for k, parts in AROUND.items():
            packed = blank
            for name, start, before, after in parts:
                middle = start + before
                both = jnp.where(line < after, tile_of(name, 2), tile_of(name, 0))
                both = pltpu.roll(both, middle % ROWS, 0) if middle % ROWS else both
                packed = jnp.where((line >= start) & (line < middle + after), both, packed)
            out[j, first + k] = packed
        return 0

    lax.fori_loop(0, ny // ROWS, surround, 0)


def kappa_of(index):
    return 0.2 * (index[0] + 1).astype(jnp.float32)


def inner_kernel(place, index, other_index, field, other, tissue, out, rows):
    core = place[0]

    def cell(group, part, comp):
        source = field if group == 0 else other
        return [lambda at, k=k: source[part, comp, core + k, at] for k in range(3)]

    masks = [lambda at, k=k: tissue[core + k, at].astype(jnp.float32) for k in (1, 2)]
    products(cell, (kappa_of(index), kappa_of(other_index)), masks, out, 0, rows)


def outer_kernel(place, index, other_index, field, other, tissue, edge, inner, out, rows):
    core = place[0]
    low, floor = core == 0, place[1] == 1
    out[:, :PLANE] = inner[...]

    def cell(group, part, comp):
        source = field if group == 0 else other

        def outside(at):
            return edge[6 * (1 - group) + 3 * part + comp, at]

        def mine(at):
            return source[part, comp, 3 * core, at]

        def inside(at):
            return source[part, comp, 1 + core, at]

        def below(at):
            return jnp.where(low, jnp.where(floor, mine(at), outside(at)), inside(at))

        return below, mine, lambda at: jnp.where(low, inside(at), outside(at))

    def here(at):
        return tissue[3 * core, at].astype(jnp.float32)

    def above(at):
        return jnp.where(low, tissue[1, at].astype(jnp.float32), edge[12, at])

    products(cell, (kappa_of(index), kappa_of(other_index)), (here, above), out, PLANE, rows)


def around_of(name):
    for tile, parts in AROUND.items():
        for other, start, before, after in parts:
            if other == name:
                return tile, start, before, after
    raise KeyError(name)


def vectors_kernel(place, mine, near, far, out):
    core = place[0]
    low = core == 0
    nx = mine.shape[-1]
    half = rows_of((ROWS, nx), 0)

    def spread(get, name):
        tile, start, before, after = around_of(name)
        main = pltpu.roll(get(MAIN[name]), 4, 0)
        side = get(tile)
        turn = (4 - before - start) % ROWS
        side = pltpu.roll(side, turn, 0) if turn else side
        head = jnp.where(half >= 4, main, jnp.where(half >= 4 - before, side, 0.0))
        tail = jnp.where(half < 4, main, jnp.where(half < 4 + after, side, 0.0))
        return jnp.concatenate([head, tail])

    def below(k):
        return jnp.where(low, far[k], near[k])

    def above(k):
        return jnp.where(low, near[k], far[k])

    sources = {
        -2: lambda k: below(PLANE + k),
        -1: below,
        0: lambda k: mine[1 - core, k],
        1: lambda k: mine[core, k],
        2: above,
        3: lambda k: above(PLANE + k),
    }
    couplings = ("z", "zy", "zx", "y", "x", "yx")
    coefs = {}
    for p in range(-1, 4):
        names = couplings[:3] if p == 3 else couplings
        coefs[p] = {n: (spread(sources[p], n + "r"), spread(sources[p], n + "i")) for n in names}
        if p < 3:
            coefs[p]["d"] = spread(sources[p], "d") + DAMPING
    v0 = {p: (spread(sources[p], "rr"), spread(sources[p], "ri")) for p in range(-2, 4)}

    def mul(c, m):
        return c[0] * m[0] - c[1] * m[1], c[0] * m[1] + c[1] * m[0]

    def conj(c, m):
        return c[0] * m[0] + c[1] * m[1], c[0] * m[1] - c[1] * m[0]

    def plus(*terms):
        return tuple(functools.reduce(lambda a, b: a + b, part) for part in zip(*terms))

    def ahead_y(x):
        return pltpu.roll(x, 2 * ROWS - 1, 0)

    def behind_y(x):
        return pltpu.roll(x, 1, 0)

    def apply(field, planes):
        stepped = {}
        flat = {}
        for p in planes + [planes[-1] + 1]:
            c, m = coefs[p], field[p]
            back = field.get(p - 1)
            my = tuple(behind_y(v) for v in m)
            mx = tuple(prv(v, 1) for v in m)
            stepped[p] = plus(conj(c["z"], m), mul(c["zy"], my), mul(c["zx"], mx))
            if p > planes[-1]:
                continue
            ys = plus(conj(c["y"], m), conj(c["zy"], back), mul(c["yx"], mx))
            xs = plus(conj(c["x"], m), conj(c["zx"], back), conj(c["yx"], my))
            flat[p] = plus(
                tuple(c["d"] * v for v in m),
                mul(c["z"], back),
                mul(c["y"], my),
                mul(c["x"], mx),
                tuple(ahead_y(v) for v in ys),
                tuple(nxt(v, 1) for v in xs),
            )
        return {p: plus(flat[p], stepped[p + 1]) for p in planes}

    v1 = apply(v0, [-1, 0, 1, 2])
    v2 = apply(v1, [0, 1])

    def own(x):
        return jnp.where(half < 4, pltpu.roll(x[:ROWS], 4, 0), pltpu.roll(x[ROWS:], 4, 0))

    held = [[[own(v[p][part]) for p in range(2)] for part in range(2)] for v in (v0, v1, v2)]
    note = jnp.zeros((ROWS, nx), jnp.float32)
    for k, (a, b) in enumerate(((0, 0), (0, 1), (1, 1), (1, 2))):
        total = sum(held[a][part][p] * held[b][part][p] for part in range(2) for p in range(2))
        note = jnp.where(half == k, jnp.sum(total, axis=0, keepdims=True), note)
    tiles = [tile for vector in held for parts in vector for tile in parts] + [note]
    for k, tile in enumerate(tiles):
        for chip in range(out.shape[0]):
            out[chip, k] = tile


def outputs_kernel(place, sums, gathered, others, modulus, residual):
    core = place[0]
    chips = gathered.shape[0]
    total = sums[0]
    for k in range(1, sums.shape[0]):
        total = total + sums[k]
    total = jnp.broadcast_to(jnp.sum(total, axis=1, keepdims=True), total.shape)
    m0, m1, m2, m3 = (total[k : k + 1] for k in range(4))
    step = m0 / m1
    norm = step * step * m2 - m0
    grown = 1.0 + norm / m0
    curve = grown * grown * m1 - 2.0 * step * grown * m2 + step * step * m3
    second = norm / curve
    shape = (chips, ROWS, total.shape[-1])
    p = jnp.broadcast_to((step + second * grown).reshape(1, 1, -1), shape)
    q = jnp.broadcast_to((step * second).reshape(1, 1, -1), shape)
    for source, first in ((gathered, 2 * core), (others, 2 - 2 * core)):
        for part in range(2):
            for plane in range(2):
                v0, v1, v2 = (source[:, 4 * k + 2 * part + plane] for k in range(3))
                flat = (chips * ROWS, shape[-1])
                modulus[part, first + plane] = (p * v0 - q * v1).reshape(flat)
                residual[part, first + plane] = (v0 - p * v1 + q * v2).reshape(flat)


def run(kernel, shapes, *arrays, scratch=(), scalars=1):
    vmem = pl.BlockSpec(memory_space=pltpu.VMEM)
    smem = pl.BlockSpec(memory_space=pltpu.SMEM)
    return pl.pallas_call(
        kernel,
        out_shape=shapes,
        in_specs=[smem] * scalars + [vmem] * (len(arrays) - scalars),
        out_specs=jax.tree.map(lambda _: vmem, shapes),
        scratch_shapes=list(scratch),
        compiler_params=pltpu.CompilerParams(vmem_limit_bytes=VMEM_BYTES),
    )(*arrays)


def body(displacement, freq_index, tissue):
    core = lax.axis_index("freq") % 2
    chips = lax.axis_size("freq") // 2
    slabs = lax.axis_size("gz")
    low = core == 0
    ny, nx = displacement.shape[-2:]
    tile = (ROWS, nx)
    place = jnp.stack([core, (low & (lax.axis_index("gz") == 0)).astype(jnp.int32)])

    def shape(*dims):
        return jax.ShapeDtypeStruct(dims, jnp.float32)

    other = swap_cores(displacement)[0]
    other_index = swap_cores(freq_index)
    field = displacement[0]

    def plane(array, k):
        return array[:, :, k].reshape(6, ny, nx)

    first, last = (
        jnp.concatenate([plane(field, k), plane(other, k), tissue[k : k + 1].astype(jnp.float32)]) for k in (0, 3)
    )
    edge = to_slabs(jnp.where(low, first, last), 1, 1)

    held = (place, freq_index, other_index, field, other, tissue)
    scratch = [pltpu.VMEM((15, ny + 2 * ROWS, nx), jnp.float32)]
    inner = run(inner_kernel, shape(chips, PLANE, *tile), *held, scratch=scratch, scalars=3)
    parts = run(outer_kernel, shape(chips, 2 * PLANE, *tile), *held, edge, inner, scratch=scratch, scalars=3)
    mine = over_chips(parts).sum(axis=0).reshape(2, PLANE, *tile)

    near = swap_cores(jnp.concatenate([mine[0], mine[1, :BEYOND]]))
    far = to_slabs(jnp.concatenate([mine[1], mine[0, :BEYOND]]), 1, 1)
    tiles = run(vectors_kernel, shape(chips, 13, *tile), place, mine, near, far)

    gathered = over_chips(tiles)
    sums = gathered[:, 12].sum(axis=0)
    sums, gathered = lax.optimization_barrier((sums + swap_cores(sums), gathered))
    others = swap_cores(gathered)
    sums = lax.all_to_all(jnp.broadcast_to(sums, (slabs, *tile)), "gz", split_axis=0, concat_axis=0, tiled=True)
    result = shape(2, 4, ny, nx)
    return tuple(run(outputs_kernel, (result, result), place, sums, gathered, others))


def solution(mesh):
    placed = (P("freq", None, None, "gz", None, None), P("freq"), P("gz", None, None))
    return jax.shard_map(
        body,
        mesh=mesh,
        in_specs=placed,
        out_specs=(P(None, "gz", None, None), P(None, "gz", None, None)),
        check_vma=False,
    )
```

```python
import functools

import jax
import jax.numpy as jnp
from jax import lax
from jax.experimental import pallas as pl
from jax.experimental.pallas import tpu as pltpu
from jax.sharding import PartitionSpec as P

DAMPING = 0.05
ROWS = 8
VMEM_BYTES = 12 << 20

NAMES = ("zr", "zi", "zyr", "zyi", "zxr", "zxi", "rr", "ri", None, None, None, "d", "yr", "yi", "xr", "xi", "yxr", "yxi", None, None)
MAIN = {name: k for k, name in enumerate(NAMES) if name}
AROUND = {
    8: (("zyr", 0, 1, 2), ("zyi", 3, 1, 2), ("zr", 6, 1, 1)),
    9: (("zi", 0, 1, 1), ("zxr", 2, 1, 1), ("zxi", 4, 1, 1), ("xi", 6, 1, 1)),
    10: (("rr", 0, 2, 2), ("ri", 4, 2, 2)),
    18: (("yr", 0, 1, 2), ("yi", 3, 1, 2), ("d", 6, 1, 1)),
    19: (("yxr", 0, 1, 2), ("yxi", 3, 1, 2), ("xr", 6, 1, 1)),
}
PLANE = len(NAMES)
BEYOND = 11


def swap_cores(array):
    pairs = [(i, i ^ 1) for i in range(lax.axis_size("freq"))]
    return lax.ppermute(array, "freq", pairs)


def to_slabs(array, first_up, cross):
    peers, slabs = lax.axis_size("freq"), lax.axis_size("gz")
    pairs = []
    for f in range(peers):
        for g in range(slabs):
            to = g + 1 if f % 2 == first_up else g - 1
            if 0 <= to < slabs:
                pairs.append((f * slabs + g, (f ^ cross) * slabs + to))
    return lax.ppermute(array, ("freq", "gz"), pairs)


def over_chips(parts):
    chips = lax.axis_size("freq") // 2
    ring = [*range(chips // 2), *reversed(range(chips // 2, chips))]
    groups = [[2 * chip + core for chip in ring] for core in range(2)]
    return lax.all_to_all(parts, "freq", split_axis=0, concat_axis=0, tiled=True, axis_index_groups=groups)


def rows_of(shape, dim):
    return lax.broadcasted_iota(jnp.int32, shape, dim)


def nxt(x, dim):
    size = x.shape[dim]
    return jnp.where(rows_of(x.shape, dim) == size - 1, 0.0, pltpu.roll(x, size - 1, dim))


def prv(x, dim):
    return jnp.where(rows_of(x.shape, dim) == 0, 0.0, pltpu.roll(x, 1, dim))


def products(cell, kappas, masks, out, first, rows):
    nx = out.shape[-1]
    ny = out.shape[0] * ROWS
    tile = (ROWS, nx)
    line, lane = rows_of(tile, 0), rows_of(tile, 1)
    blank = jnp.zeros(tile, jnp.float32)

    last = ny // ROWS - 1

    def at(read, j):
        return read(pl.ds(pl.multiple_of(ROWS * j, ROWS), ROWS))

    def next_y(read, j, own):
        after = jnp.where(j == last, 0.0, at(read, jnp.minimum(j + 1, last)))
        return pltpu.roll(jnp.where(line == 0, after, own), ROWS - 1, 0)

    def prev_y(read, j, own):
        before = at(read, jnp.maximum(j - 1, 0))
        return pltpu.roll(jnp.where(line == ROWS - 1, before, own), 1, 0)

    def re(a, b):
        return a[0] * b[0] + a[1] * b[1]

    def im(a, b):
        return a[0] * b[1] - a[1] * b[0]

    names = [name for name in NAMES if name]
    for k in range(len(names)):
        rows[k, :ROWS] = blank
        rows[k, ROWS + ny :] = blank
    def chunk(j, _):
        here, above = (at(mask, j) for mask in masks)
        here_y, here_x = next_y(masks[0], j, here), nxt(here, 1)
        bottom = (line == 0) & (j == 0)
        sums = None
        for group in range(2):
            scales = [m * kappas[group] for m in (here, above, here_y, here_x)]
            for comp in range(3):
                gz, gp, gy, gx, hy, hx, s, t = ([] for _ in range(8))
                for part in range(2):
                    below, mine, up = cell(group, part, comp)
                    u, uz = at(mine, j), at(up, j)
                    uy, ux = next_y(mine, j, u), nxt(u, 1)
                    gz.append(uz - u)
                    gp.append(u - at(below, j))
                    gy.append(uy - u)
                    gx.append(ux - u)
                    hy.append(jnp.where(bottom, 0.0, u - prev_y(mine, j, u)))
                    hx.append(jnp.where(lane == 0, 0.0, u - pltpu.roll(u, 1, 1)))
                    s.append(gz[-1] + gy[-1] + gx[-1])
                    t.append([u * scales[0], uz * scales[1], uy * scales[2], ux * scales[3]])
                new = [re(s, s), re(gz, gz), re(gy, gy), re(gx, gx)]
                for a, b in ((s, gp), (s, hy), (s, hx), (gp, hy), (gp, hx), (hy, hx)):
                    new += [re(a, b), im(a, b)]
                ts = [[t[0][k], t[1][k]] for k in range(4)]
                for f in (re, im):
                    new.append(f(gz, ts[1]) + f(gy, ts[2]) + f(gx, ts[3]) - f(s, ts[0]))
                sums = new if sums is None else [old + value for old, value in zip(sums, new)]
        done = {"d": here * sums[0] + above * sums[1] + here_y * sums[2] + here_x * sums[3]}
        for k, name in enumerate(("z", "y", "x", "zy", "zx", "yx")):
            signed = -here if k < 3 else here
            done[name + "r"] = signed * sums[4 + 2 * k]
            done[name + "i"] = signed * sums[5 + 2 * k]
        done["rr"], done["ri"] = sums[16], sums[17]
        for k, name in enumerate(names):
            out[j, first + MAIN[name]] = done[name]
            rows[k, pl.ds(pl.multiple_of(ROWS * j + ROWS, ROWS), ROWS)] = done[name]
        return 0

    lax.fori_loop(0, ny // ROWS, chunk, 0)

    def surround(j, _):
        def tile_of(name, k):
            return rows[names.index(name), pl.ds(pl.multiple_of(ROWS * (j + k), ROWS), ROWS)]

        for k, parts in AROUND.items():
            packed = blank
            for name, start, before, after in parts:
                middle = start + before
                both = jnp.where(line < after, tile_of(name, 2), tile_of(name, 0))
                both = pltpu.roll(both, middle % ROWS, 0) if middle % ROWS else both
                packed = jnp.where((line >= start) & (line < middle + after), both, packed)
            out[j, first + k] = packed
        return 0

    lax.fori_loop(0, ny // ROWS, surround, 0)


def kappa_of(index):
    return 0.2 * (index[0] + 1).astype(jnp.float32)


def inner_kernel(place, index, other_index, field, other, tissue, out, rows):
    core = place[0]

    def cell(group, part, comp):
        source = field if group == 0 else other
        return [lambda at, k=k: source[part, comp, core + k, at] for k in range(3)]

    masks = [lambda at, k=k: tissue[core + k, at].astype(jnp.float32) for k in (1, 2)]
    products(cell, (kappa_of(index), kappa_of(other_index)), masks, out, 0, rows)


def outer_kernel(place, index, other_index, field, other, tissue, edge, inner, out, rows):
    core = place[0]
    low, floor = core == 0, place[1] == 1
    out[:, :PLANE] = inner[...]

    def cell(group, part, comp):
        source = field if group == 0 else other

        def outside(at):
            return edge[6 * (1 - group) + 3 * part + comp, at]

        def mine(at):
            return source[part, comp, 3 * core, at]

        def inside(at):
            return source[part, comp, 1 + core, at]

        def below(at):
            return jnp.where(low, jnp.where(floor, mine(at), outside(at)), inside(at))

        return below, mine, lambda at: jnp.where(low, inside(at), outside(at))

    def here(at):
        return tissue[3 * core, at].astype(jnp.float32)

    def above(at):
        return jnp.where(low, tissue[1, at].astype(jnp.float32), edge[12, at])

    products(cell, (kappa_of(index), kappa_of(other_index)), (here, above), out, PLANE, rows)


def around_of(name):
    for tile, parts in AROUND.items():
        for other, start, before, after in parts:
            if other == name:
                return tile, start, before, after
    raise KeyError(name)


def vectors_kernel(place, mine, near, far, out):
    core = place[0]
    low = core == 0
    nx = mine.shape[-1]
    half = rows_of((ROWS, nx), 0)

    def spread(get, name):
        tile, start, before, after = around_of(name)
        main = pltpu.roll(get(MAIN[name]), 4, 0)
        side = get(tile)
        turn = (4 - before - start) % ROWS
        side = pltpu.roll(side, turn, 0) if turn else side
        head = jnp.where(half >= 4, main, jnp.where(half >= 4 - before, side, 0.0))
        tail = jnp.where(half < 4, main, jnp.where(half < 4 + after, side, 0.0))
        return jnp.concatenate([head, tail])

    def below(k):
        return jnp.where(low, far[k], near[k])

    def above(k):
        return jnp.where(low, near[k], far[k])

    sources = {
        -2: lambda k: below(PLANE + k),
        -1: below,
        0: lambda k: mine[1 - core, k],
        1: lambda k: mine[core, k],
        2: above,
        3: lambda k: above(PLANE + k),
    }
    couplings = ("z", "zy", "zx", "y", "x", "yx")
    coefs = {}
    for p in range(-1, 4):
        names = couplings[:3] if p == 3 else couplings
        coefs[p] = {n: (spread(sources[p], n + "r"), spread(sources[p], n + "i")) for n in names}
        if p < 3:
            coefs[p]["d"] = spread(sources[p], "d") + DAMPING
    v0 = {p: (spread(sources[p], "rr"), spread(sources[p], "ri")) for p in range(-2, 4)}

    def mul(c, m):
        return c[0] * m[0] - c[1] * m[1], c[0] * m[1] + c[1] * m[0]

    def conj(c, m):
        return c[0] * m[0] + c[1] * m[1], c[0] * m[1] - c[1] * m[0]

    def plus(*terms):
        return tuple(functools.reduce(lambda a, b: a + b, part) for part in zip(*terms))

    def ahead_y(x):
        return pltpu.roll(x, 2 * ROWS - 1, 0)

    def behind_y(x):
        return pltpu.roll(x, 1, 0)

    def apply(field, planes):
        stepped = {}
        flat = {}
        for p in planes + [planes[-1] + 1]:
            c, m = coefs[p], field[p]
            back = field.get(p - 1)
            my = tuple(behind_y(v) for v in m)
            mx = tuple(prv(v, 1) for v in m)
            stepped[p] = plus(conj(c["z"], m), mul(c["zy"], my), mul(c["zx"], mx))
            if p > planes[-1]:
                continue
            ys = plus(conj(c["y"], m), conj(c["zy"], back), mul(c["yx"], mx))
            xs = plus(conj(c["x"], m), conj(c["zx"], back), conj(c["yx"], my))
            flat[p] = plus(
                tuple(c["d"] * v for v in m),
                mul(c["z"], back),
                mul(c["y"], my),
                mul(c["x"], mx),
                tuple(ahead_y(v) for v in ys),
                tuple(nxt(v, 1) for v in xs),
            )
        return {p: plus(flat[p], stepped[p + 1]) for p in planes}

    v1 = apply(v0, [-1, 0, 1, 2])
    v2 = apply(v1, [0, 1])

    def own(x):
        return jnp.where(half < 4, pltpu.roll(x[:ROWS], 4, 0), pltpu.roll(x[ROWS:], 4, 0))

    held = [[[own(v[p][part]) for p in range(2)] for part in range(2)] for v in (v0, v1, v2)]
    note = jnp.zeros((ROWS, nx), jnp.float32)
    for k, (a, b) in enumerate(((0, 0), (0, 1), (1, 1), (1, 2))):
        total = sum(held[a][part][p] * held[b][part][p] for part in range(2) for p in range(2))
        note = jnp.where(half == k, jnp.sum(total, axis=0, keepdims=True), note)
    tiles = [tile for vector in held for parts in vector for tile in parts] + [note]
    for k, tile in enumerate(tiles):
        for chip in range(out.shape[0]):
            out[chip, k] = tile


def outputs_kernel(place, sums, gathered, others, modulus, residual):
    core = place[0]
    chips = gathered.shape[0]
    total = sums[0]
    for k in range(1, sums.shape[0]):
        total = total + sums[k]
    total = jnp.broadcast_to(jnp.sum(total, axis=1, keepdims=True), total.shape)
    m0, m1, m2, m3 = (total[k : k + 1] for k in range(4))
    step = m0 / m1
    norm = step * step * m2 - m0
    grown = 1.0 + norm / m0
    curve = grown * grown * m1 - 2.0 * step * grown * m2 + step * step * m3
    second = norm / curve
    shape = (chips, ROWS, total.shape[-1])
    p = jnp.broadcast_to((step + second * grown).reshape(1, 1, -1), shape)
    q = jnp.broadcast_to((step * second).reshape(1, 1, -1), shape)
    for source, first in ((gathered, 2 * core), (others, 2 - 2 * core)):
        for part in range(2):
            for plane in range(2):
                v0, v1, v2 = (source[:, 4 * k + 2 * part + plane] for k in range(3))
                flat = (chips * ROWS, shape[-1])
                modulus[part, first + plane] = (p * v0 - q * v1).reshape(flat)
                residual[part, first + plane] = (v0 - p * v1 + q * v2).reshape(flat)


def run(kernel, shapes, *arrays, scratch=(), scalars=1):
    vmem = pl.BlockSpec(memory_space=pltpu.VMEM)
    smem = pl.BlockSpec(memory_space=pltpu.SMEM)
    return pl.pallas_call(
        kernel,
        out_shape=shapes,
        in_specs=[smem] * scalars + [vmem] * (len(arrays) - scalars),
        out_specs=jax.tree.map(lambda _: vmem, shapes),
        scratch_shapes=list(scratch),
        compiler_params=pltpu.CompilerParams(vmem_limit_bytes=VMEM_BYTES),
    )(*arrays)


def body(displacement, freq_index, tissue):
    core = lax.axis_index("freq") % 2
    chips = lax.axis_size("freq") // 2
    slabs = lax.axis_size("gz")
    low = core == 0
    ny, nx = displacement.shape[-2:]
    tile = (ROWS, nx)
    place = jnp.stack([core, (low & (lax.axis_index("gz") == 0)).astype(jnp.int32)])

    def shape(*dims):
        return jax.ShapeDtypeStruct(dims, jnp.float32)

    other = swap_cores(displacement)[0]
    other_index = swap_cores(freq_index)
    field = displacement[0]

    def plane(array, k):
        return array[:, :, k].reshape(6, ny, nx)

    first, last = (
        jnp.concatenate([plane(field, k), plane(other, k), tissue[k : k + 1].astype(jnp.float32)]) for k in (0, 3)
    )
    edge = to_slabs(jnp.where(low, first, last), 1, 1)

    held = (place, freq_index, other_index, field, other, tissue)
    scratch = [pltpu.VMEM((15, ny + 2 * ROWS, nx), jnp.float32)]
    inner = run(inner_kernel, shape(chips, PLANE, *tile), *held, scratch=scratch, scalars=3)
    parts = run(outer_kernel, shape(chips, 2 * PLANE, *tile), *held, edge, inner, scratch=scratch, scalars=3)
    mine = over_chips(parts).sum(axis=0).reshape(2, PLANE, *tile)

    near = swap_cores(jnp.concatenate([mine[0], mine[1, :BEYOND]]))
    far = to_slabs(jnp.concatenate([mine[1], mine[0, :BEYOND]]), 1, 1)
    tiles = run(vectors_kernel, shape(chips, 13, *tile), place, mine, near, far)

    gathered = over_chips(tiles)
    sums = gathered[:, 12].sum(axis=0)
    sums, gathered = lax.optimization_barrier((sums + swap_cores(sums), gathered))
    others = swap_cores(gathered)
    sums = lax.all_to_all(jnp.broadcast_to(sums, (slabs, *tile)), "gz", split_axis=0, concat_axis=0, tiled=True)
    result = shape(2, 4, ny, nx)
    return tuple(run(outputs_kernel, (result, result), place, sums, gathered, others))


def solution(mesh):
    placed = (P("freq", None, None, "gz", None, None), P("freq"), P("gz", None, None))
    return jax.shard_map(
        body,
        mesh=mesh,
        in_specs=placed,
        out_specs=(P(None, "gz", None, None), P(None, "gz", None, None)),
        check_vma=False,
    )
```

```python
import functools

import jax
import jax.numpy as jnp
from jax import lax
from jax.experimental import pallas as pl
from jax.experimental.pallas import tpu as pltpu
from jax.sharding import PartitionSpec as P

DAMPING = 0.05
ROWS = 8
VMEM_BYTES = 12 << 20

NAMES = ("zr", "zi", "zyr", "zyi", "zxr", "zxi", "rr", "ri", None, None, None, "d", "yr", "yi", "xr", "xi", "yxr", "yxi", None, None)
MAIN = {name: k for k, name in enumerate(NAMES) if name}
AROUND = {
    8: (("zyr", 0, 1, 2), ("zyi", 3, 1, 2), ("zr", 6, 1, 1)),
    9: (("zi", 0, 1, 1), ("zxr", 2, 1, 1), ("zxi", 4, 1, 1), ("xi", 6, 1, 1)),
    10: (("rr", 0, 2, 2), ("ri", 4, 2, 2)),
    18: (("yr", 0, 1, 2), ("yi", 3, 1, 2), ("d", 6, 1, 1)),
    19: (("yxr", 0, 1, 2), ("yxi", 3, 1, 2), ("xr", 6, 1, 1)),
}
PLANE = len(NAMES)
BEYOND = 11


def swap_cores(array):
    pairs = [(i, i ^ 1) for i in range(lax.axis_size("freq"))]
    return lax.ppermute(array, "freq", pairs)


def to_slabs(array, first_up, cross):
    peers, slabs = lax.axis_size("freq"), lax.axis_size("gz")
    pairs = []
    for f in range(peers):
        for g in range(slabs):
            to = g + 1 if f % 2 == first_up else g - 1
            if 0 <= to < slabs:
                pairs.append((f * slabs + g, (f ^ cross) * slabs + to))
    return lax.ppermute(array, ("freq", "gz"), pairs)


def over_chips(parts):
    peers = lax.axis_size("freq")
    groups = [list(range(core, peers, 2)) for core in range(2)]
    return lax.all_to_all(parts, "freq", split_axis=0, concat_axis=0, tiled=True, axis_index_groups=groups)


def rows_of(shape, dim):
    return lax.broadcasted_iota(jnp.int32, shape, dim)


def nxt(x, dim):
    size = x.shape[dim]
    return jnp.where(rows_of(x.shape, dim) == size - 1, 0.0, pltpu.roll(x, size - 1, dim))


def prv(x, dim):
    return jnp.where(rows_of(x.shape, dim) == 0, 0.0, pltpu.roll(x, 1, dim))


def products(cell, kappas, masks, out, first, rows):
    nx = out.shape[-1]
    ny = out.shape[0] * ROWS
    tile = (ROWS, nx)
    line, lane = rows_of(tile, 0), rows_of(tile, 1)
    blank = jnp.zeros(tile, jnp.float32)

    def at(read, j):
        return read(pl.ds(ROWS * j, ROWS))

    def next_y(read, j):
        if ROWS * j + ROWS < ny:
            return read(pl.ds(ROWS * j + 1, ROWS))
        return jnp.where(line == ROWS - 1, 0.0, pltpu.roll(at(read, j), ROWS - 1, 0))

    def prev_y(read, j):
        if j:
            return read(pl.ds(ROWS * j - 1, ROWS))
        return pltpu.roll(at(read, j), 1, 0)

    def re(a, b):
        return a[0] * b[0] + a[1] * b[1]

    def im(a, b):
        return a[0] * b[1] - a[1] * b[0]

    names = [name for name in NAMES if name]
    for k in range(len(names)):
        rows[k, :ROWS] = blank
        rows[k, ROWS + ny :] = blank
    for j in range(ny // ROWS):
        here, above = (at(mask, j) for mask in masks)
        here_y, here_x = next_y(masks[0], j), nxt(here, 1)
        sums = None
        for group in range(2):
            scales = [m * kappas[group] for m in (here, above, here_y, here_x)]
            for comp in range(3):
                gz, gp, gy, gx, hy, hx, s, t = ([] for _ in range(8))
                for part in range(2):
                    below, mine, up = cell(group, part, comp)
                    u, uz = at(mine, j), at(up, j)
                    uy, ux = next_y(mine, j), nxt(u, 1)
                    gz.append(uz - u)
                    gp.append(u - at(below, j))
                    gy.append(uy - u)
                    gx.append(ux - u)
                    step = u - prev_y(mine, j)
                    hy.append(step if j else jnp.where(line == 0, 0.0, step))
                    hx.append(jnp.where(lane == 0, 0.0, u - pltpu.roll(u, 1, 1)))
                    s.append(gz[-1] + gy[-1] + gx[-1])
                    t.append([u * scales[0], uz * scales[1], uy * scales[2], ux * scales[3]])
                new = [re(s, s), re(gz, gz), re(gy, gy), re(gx, gx)]
                for a, b in ((s, gp), (s, hy), (s, hx), (gp, hy), (gp, hx), (hy, hx)):
                    new += [re(a, b), im(a, b)]
                ts = [[t[0][k], t[1][k]] for k in range(4)]
                for f in (re, im):
                    new.append(f(gz, ts[1]) + f(gy, ts[2]) + f(gx, ts[3]) - f(s, ts[0]))
                sums = new if sums is None else [old + value for old, value in zip(sums, new)]
        done = {"d": here * sums[0] + above * sums[1] + here_y * sums[2] + here_x * sums[3]}
        for k, name in enumerate(("z", "y", "x", "zy", "zx", "yx")):
            signed = -here if k < 3 else here
            done[name + "r"] = signed * sums[4 + 2 * k]
            done[name + "i"] = signed * sums[5 + 2 * k]
        done["rr"], done["ri"] = sums[16], sums[17]
        for k, name in enumerate(names):
            out[j, first + MAIN[name]] = done[name]
            rows[k, ROWS + ROWS * j : 2 * ROWS + ROWS * j] = done[name]
    for j in range(ny // ROWS):
        for k, parts in AROUND.items():
            packed = blank
            for name, start, before, after in parts:
                kept = names.index(name)
                middle = start + before
                head = rows[kept, pl.ds(ROWS + ROWS * j - middle, ROWS)]
                tail = rows[kept, pl.ds(2 * ROWS + ROWS * j - middle, ROWS)]
                packed = jnp.where((line >= start) & (line < middle), head, packed)
                packed = jnp.where((line >= middle) & (line < middle + after), tail, packed)
            out[j, first + k] = packed


def kappa_of(index):
    return 0.2 * (index[0] + 1).astype(jnp.float32)


def inner_kernel(place, index, other_index, field, other, tissue, out, rows):
    core = place[0]

    def cell(group, part, comp):
        source = field if group == 0 else other
        return [lambda at, k=k: source[part, comp, core + k, at] for k in range(3)]

    masks = [lambda at, k=k: tissue[core + k, at].astype(jnp.float32) for k in (1, 2)]
    products(cell, (kappa_of(index), kappa_of(other_index)), masks, out, 0, rows)


def outer_kernel(place, index, other_index, field, other, tissue, same, cross, inner, out, rows):
    core = place[0]
    low, floor = core == 0, place[1] == 1
    out[:, :PLANE] = inner[...]

    def cell(group, part, comp):
        source = field if group == 0 else other

        def outside(at):
            return (same, cross)[group][3 * part + comp, at]

        def mine(at):
            return source[part, comp, 3 * core, at]

        def inside(at):
            return source[part, comp, 1 + core, at]

        def below(at):
            return jnp.where(low, jnp.where(floor, mine(at), outside(at)), inside(at))

        return below, mine, lambda at: jnp.where(low, inside(at), outside(at))

    def here(at):
        return tissue[3 * core, at].astype(jnp.float32)

    def above(at):
        return jnp.where(low, tissue[1, at].astype(jnp.float32), cross[6, at])

    products(cell, (kappa_of(index), kappa_of(other_index)), (here, above), out, PLANE, rows)


def around_of(name):
    for tile, parts in AROUND.items():
        for other, start, before, after in parts:
            if other == name:
                return tile, start, before, after
    raise KeyError(name)


def vectors_kernel(place, mine, near, far, out):
    core = place[0]
    low = core == 0
    nx = mine.shape[-1]
    half = rows_of((ROWS, nx), 0)

    def spread(get, name):
        tile, start, before, after = around_of(name)
        main = pltpu.roll(get(MAIN[name]), 4, 0)
        side = get(tile)
        turn = (4 - before - start) % ROWS
        side = pltpu.roll(side, turn, 0) if turn else side
        head = jnp.where(half >= 4, main, jnp.where(half >= 4 - before, side, 0.0))
        tail = jnp.where(half < 4, main, jnp.where(half < 4 + after, side, 0.0))
        return jnp.concatenate([head, tail])

    def below(k):
        return jnp.where(low, far[k], near[k])

    def above(k):
        return jnp.where(low, near[k], far[k])

    sources = {
        -2: lambda k: below(PLANE + k),
        -1: below,
        0: lambda k: mine[1 - core, k],
        1: lambda k: mine[core, k],
        2: above,
        3: lambda k: above(PLANE + k),
    }
    couplings = ("z", "zy", "zx", "y", "x", "yx")
    coefs = {}
    for p in range(-1, 4):
        names = couplings[:3] if p == 3 else couplings
        coefs[p] = {n: (spread(sources[p], n + "r"), spread(sources[p], n + "i")) for n in names}
        if p < 3:
            coefs[p]["d"] = spread(sources[p], "d") + DAMPING
    v0 = {p: (spread(sources[p], "rr"), spread(sources[p], "ri")) for p in range(-2, 4)}

    def mul(c, m):
        return c[0] * m[0] - c[1] * m[1], c[0] * m[1] + c[1] * m[0]

    def conj(c, m):
        return c[0] * m[0] + c[1] * m[1], c[0] * m[1] - c[1] * m[0]

    def plus(*terms):
        return tuple(functools.reduce(lambda a, b: a + b, part) for part in zip(*terms))

    def ahead_y(x):
        return pltpu.roll(x, 2 * ROWS - 1, 0)

    def behind_y(x):
        return pltpu.roll(x, 1, 0)

    def apply(field, planes):
        stepped = {}
        flat = {}
        for p in planes + [planes[-1] + 1]:
            c, m = coefs[p], field[p]
            back = field.get(p - 1)
            my = tuple(behind_y(v) for v in m)
            mx = tuple(prv(v, 1) for v in m)
            stepped[p] = plus(conj(c["z"], m), mul(c["zy"], my), mul(c["zx"], mx))
            if p > planes[-1]:
                continue
            ys = plus(conj(c["y"], m), conj(c["zy"], back), mul(c["yx"], mx))
            xs = plus(conj(c["x"], m), conj(c["zx"], back), conj(c["yx"], my))
            flat[p] = plus(
                tuple(c["d"] * v for v in m),
                mul(c["z"], back),
                mul(c["y"], my),
                mul(c["x"], mx),
                tuple(ahead_y(v) for v in ys),
                tuple(nxt(v, 1) for v in xs),
            )
        return {p: plus(flat[p], stepped[p + 1]) for p in planes}

    v1 = apply(v0, [-1, 0, 1, 2])
    v2 = apply(v1, [0, 1])

    def own(x):
        return jnp.where(half < 4, pltpu.roll(x[:ROWS], 4, 0), pltpu.roll(x[ROWS:], 4, 0))

    held = [[[own(v[p][part]) for p in range(2)] for part in range(2)] for v in (v0, v1, v2)]
    note = jnp.zeros((ROWS, nx), jnp.float32)
    for k, (a, b) in enumerate(((0, 0), (0, 1), (1, 1), (1, 2))):
        total = sum(held[a][part][p] * held[b][part][p] for part in range(2) for p in range(2))
        note = jnp.where(half == k, jnp.sum(total, axis=0, keepdims=True), note)
    tiles = [tile for vector in held for parts in vector for tile in parts] + [note]
    for k, tile in enumerate(tiles):
        for chip in range(out.shape[0]):
            out[chip, k] = tile


def outputs_kernel(place, sums, gathered, others, modulus, residual):
    core = place[0]
    chips = gathered.shape[0]
    total = sums[0]
    for k in range(1, sums.shape[0]):
        total = total + sums[k]
    total = jnp.broadcast_to(jnp.sum(total, axis=1, keepdims=True), total.shape)
    m0, m1, m2, m3 = (total[k : k + 1] for k in range(4))
    step = m0 / m1
    norm = step * step * m2 - m0
    grown = 1.0 + norm / m0
    curve = grown * grown * m1 - 2.0 * step * grown * m2 + step * step * m3
    second = norm / curve
    shape = (chips, ROWS, total.shape[-1])
    p = jnp.broadcast_to((step + second * grown).reshape(1, 1, -1), shape)
    q = jnp.broadcast_to((step * second).reshape(1, 1, -1), shape)
    for source, first in ((gathered, 2 * core), (others, 2 - 2 * core)):
        for part in range(2):
            for plane in range(2):
                v0, v1, v2 = (source[:, 4 * k + 2 * part + plane] for k in range(3))
                flat = (chips * ROWS, shape[-1])
                modulus[part, first + plane] = (p * v0 - q * v1).reshape(flat)
                residual[part, first + plane] = (v0 - p * v1 + q * v2).reshape(flat)


def run(kernel, shapes, *arrays, scratch=(), scalars=1):
    vmem = pl.BlockSpec(memory_space=pltpu.VMEM)
    smem = pl.BlockSpec(memory_space=pltpu.SMEM)
    return pl.pallas_call(
        kernel,
        out_shape=shapes,
        in_specs=[smem] * scalars + [vmem] * (len(arrays) - scalars),
        out_specs=jax.tree.map(lambda _: vmem, shapes),
        scratch_shapes=list(scratch),
        compiler_params=pltpu.CompilerParams(vmem_limit_bytes=VMEM_BYTES),
    )(*arrays)


def body(displacement, freq_index, tissue):
    core = lax.axis_index("freq") % 2
    chips = lax.axis_size("freq") // 2
    slabs = lax.axis_size("gz")
    low = core == 0
    ny, nx = displacement.shape[-2:]
    tile = (ROWS, nx)
    place = jnp.stack([core, (low & (lax.axis_index("gz") == 0)).astype(jnp.int32)])

    def shape(*dims):
        return jax.ShapeDtypeStruct(dims, jnp.float32)

    field = displacement[0]
    first, last = (field[:, :, k].reshape(6, ny, nx) for k in (0, 3))
    same = to_slabs(jnp.where(low, last, first), 0, 0)
    cross = to_slabs(jnp.concatenate([jnp.where(low, first, last), tissue[:1].astype(jnp.float32)]), 1, 1)
    other = swap_cores(displacement)[0]
    other_index = swap_cores(freq_index)

    held = (place, freq_index, other_index, field, other, tissue)
    scratch = [pltpu.VMEM((15, ny + 2 * ROWS, nx), jnp.float32)]
    inner = run(inner_kernel, shape(chips, PLANE, *tile), *held, scratch=scratch, scalars=3)
    parts = run(outer_kernel, shape(chips, 2 * PLANE, *tile), *held, same, cross, inner, scratch=scratch, scalars=3)
    mine = over_chips(parts).sum(axis=0).reshape(2, PLANE, *tile)

    near = swap_cores(jnp.concatenate([mine[0], mine[1, :BEYOND]]))
    far = to_slabs(jnp.concatenate([mine[1], mine[0, :BEYOND]]), 1, 1)
    tiles = run(vectors_kernel, shape(chips, 13, *tile), place, mine, near, far)

    gathered = over_chips(tiles)
    sums = gathered[:, 12].sum(axis=0)
    sums, gathered = lax.optimization_barrier((sums + swap_cores(sums), gathered))
    others = swap_cores(gathered)
    sums = lax.all_to_all(jnp.broadcast_to(sums, (slabs, *tile)), "gz", split_axis=0, concat_axis=0, tiled=True)
    result = shape(2, 4, ny, nx)
    return tuple(run(outputs_kernel, (result, result), place, sums, gathered, others))


def solution(mesh):
    placed = (P("freq", None, None, "gz", None, None), P("freq"), P("gz", None, None))
    return jax.shard_map(
        body,
        mesh=mesh,
        in_specs=placed,
        out_specs=(P(None, "gz", None, None), P(None, "gz", None, None)),
        check_vma=False,
    )
```

```python
import functools

import jax
import jax.numpy as jnp
from jax import lax
from jax.experimental import pallas as pl
from jax.experimental.pallas import tpu as pltpu
from jax.sharding import PartitionSpec as P

DAMPING = 0.05
ROWS = 8
VMEM_BYTES = 12 << 20

NAMES = ("zr", "zi", "zyr", "zyi", "zxr", "zxi", "rr", "ri", None, None, None, "d", "yr", "yi", "xr", "xi", "yxr", "yxi", None, None)
MAIN = {name: k for k, name in enumerate(NAMES) if name}
AROUND = {
    8: (("zyr", 0, 1, 2), ("zyi", 3, 1, 2), ("zr", 6, 1, 1)),
    9: (("zi", 0, 1, 1), ("zxr", 2, 1, 1), ("zxi", 4, 1, 1), ("xi", 6, 1, 1)),
    10: (("rr", 0, 2, 2), ("ri", 4, 2, 2)),
    18: (("yr", 0, 1, 2), ("yi", 3, 1, 2), ("d", 6, 1, 1)),
    19: (("yxr", 0, 1, 2), ("yxi", 3, 1, 2), ("xr", 6, 1, 1)),
}
PLANE = len(NAMES)
BEYOND = 11


def swap_cores(array):
    pairs = [(i, i ^ 1) for i in range(lax.axis_size("freq"))]
    return lax.ppermute(array, "freq", pairs)


def to_slabs(array, first_up, cross):
    peers, slabs = lax.axis_size("freq"), lax.axis_size("gz")
    pairs = []
    for f in range(peers):
        for g in range(slabs):
            to = g + 1 if f % 2 == first_up else g - 1
            if 0 <= to < slabs:
                pairs.append((f * slabs + g, (f ^ cross) * slabs + to))
    return lax.ppermute(array, ("freq", "gz"), pairs)


def over_chips(parts):
    peers = lax.axis_size("freq")
    groups = [list(range(core, peers, 2)) for core in range(2)]
    return lax.all_to_all(parts, "freq", split_axis=0, concat_axis=0, tiled=True, axis_index_groups=groups)


def rows_of(shape, dim):
    return lax.broadcasted_iota(jnp.int32, shape, dim)


def nxt(x, dim):
    size = x.shape[dim]
    return jnp.where(rows_of(x.shape, dim) == size - 1, 0.0, pltpu.roll(x, size - 1, dim))


def prv(x, dim):
    return jnp.where(rows_of(x.shape, dim) == 0, 0.0, pltpu.roll(x, 1, dim))


def products(cell, kappas, masks, out, first, rows):
    nx = out.shape[-1]
    ny = out.shape[0] * ROWS
    tile = (ROWS, nx)
    line, lane = rows_of(tile, 0), rows_of(tile, 1)
    blank = jnp.zeros(tile, jnp.float32)

    def at(read, j):
        return read(pl.ds(ROWS * j, ROWS))

    def next_y(read, j):
        if ROWS * j + ROWS < ny:
            return read(pl.ds(ROWS * j + 1, ROWS))
        return jnp.where(line == ROWS - 1, 0.0, pltpu.roll(at(read, j), ROWS - 1, 0))

    def prev_y(read, j):
        if j:
            return read(pl.ds(ROWS * j - 1, ROWS))
        return pltpu.roll(at(read, j), 1, 0)

    def re(a, b):
        return a[0] * b[0] + a[1] * b[1]

    def im(a, b):
        return a[0] * b[1] - a[1] * b[0]

    names = [name for name in NAMES if name]
    for k in range(len(names)):
        rows[k, :ROWS] = blank
        rows[k, ROWS + ny :] = blank
    for j in range(ny // ROWS):
        here, above = (at(mask, j) for mask in masks)
        here_y, here_x = next_y(masks[0], j), nxt(here, 1)
        sums = None
        for group in range(2):
            scales = [m * kappas[group] for m in (here, above, here_y, here_x)]
            for comp in range(3):
                gz, gp, gy, gx, hy, hx, s, t = ([] for _ in range(8))
                for part in range(2):
                    below, mine, up = cell(group, part, comp)
                    u, uz = at(mine, j), at(up, j)
                    uy, ux = next_y(mine, j), nxt(u, 1)
                    gz.append(uz - u)
                    gp.append(u - at(below, j))
                    gy.append(uy - u)
                    gx.append(ux - u)
                    step = u - prev_y(mine, j)
                    hy.append(step if j else jnp.where(line == 0, 0.0, step))
                    hx.append(jnp.where(lane == 0, 0.0, u - pltpu.roll(u, 1, 1)))
                    s.append(gz[-1] + gy[-1] + gx[-1])
                    t.append([u * scales[0], uz * scales[1], uy * scales[2], ux * scales[3]])
                new = [re(s, s), re(gz, gz), re(gy, gy), re(gx, gx)]
                for a, b in ((s, gp), (s, hy), (s, hx), (gp, hy), (gp, hx), (hy, hx)):
                    new += [re(a, b), im(a, b)]
                ts = [[t[0][k], t[1][k]] for k in range(4)]
                for f in (re, im):
                    new.append(f(gz, ts[1]) + f(gy, ts[2]) + f(gx, ts[3]) - f(s, ts[0]))
                sums = new if sums is None else [old + value for old, value in zip(sums, new)]
        done = {"d": here * sums[0] + above * sums[1] + here_y * sums[2] + here_x * sums[3]}
        for k, name in enumerate(("z", "y", "x", "zy", "zx", "yx")):
            signed = -here if k < 3 else here
            done[name + "r"] = signed * sums[4 + 2 * k]
            done[name + "i"] = signed * sums[5 + 2 * k]
        done["rr"], done["ri"] = sums[16], sums[17]
        for k, name in enumerate(names):
            out[j, first + MAIN[name]] = done[name]
            rows[k, ROWS + ROWS * j : 2 * ROWS + ROWS * j] = done[name]
    for j in range(ny // ROWS):
        for k, parts in AROUND.items():
            packed = blank
            for name, start, before, after in parts:
                kept = names.index(name)
                middle = start + before
                head = rows[kept, pl.ds(ROWS + ROWS * j - middle, ROWS)]
                tail = rows[kept, pl.ds(2 * ROWS + ROWS * j - middle, ROWS)]
                packed = jnp.where((line >= start) & (line < middle), head, packed)
                packed = jnp.where((line >= middle) & (line < middle + after), tail, packed)
            out[j, first + k] = packed


def kappa_of(index):
    return 0.2 * (index[0] + 1).astype(jnp.float32)


def inner_kernel(place, index, other_index, field, other, tissue, out, rows):
    core = place[0]

    def cell(group, part, comp):
        source = field if group == 0 else other
        return [lambda at, k=k: source[part, comp, core + k, at] for k in range(3)]

    masks = [lambda at, k=k: tissue[core + k, at].astype(jnp.float32) for k in (1, 2)]
    products(cell, (kappa_of(index), kappa_of(other_index)), masks, out, 0, rows)


def outer_kernel(place, index, other_index, field, other, tissue, same, cross, inner, out, rows):
    core = place[0]
    low, floor = core == 0, place[1] == 1
    out[:, :PLANE] = inner[...]

    def cell(group, part, comp):
        source = field if group == 0 else other

        def outside(at):
            return (same, cross)[group][3 * part + comp, at]

        def mine(at):
            return source[part, comp, 3 * core, at]

        def inside(at):
            return source[part, comp, 1 + core, at]

        def below(at):
            return jnp.where(low, jnp.where(floor, mine(at), outside(at)), inside(at))

        return below, mine, lambda at: jnp.where(low, inside(at), outside(at))

    def here(at):
        return tissue[3 * core, at].astype(jnp.float32)

    def above(at):
        return jnp.where(low, tissue[1, at].astype(jnp.float32), cross[6, at])

    products(cell, (kappa_of(index), kappa_of(other_index)), (here, above), out, PLANE, rows)


def around_of(name):
    for tile, parts in AROUND.items():
        for other, start, before, after in parts:
            if other == name:
                return tile, start, before, after
    raise KeyError(name)


def vectors_kernel(place, mine, near, far, out):
    core = place[0]
    low = core == 0
    nx = mine.shape[-1]
    half = rows_of((ROWS, nx), 0)

    def spread(get, name):
        tile, start, before, after = around_of(name)
        main = pltpu.roll(get(MAIN[name]), 4, 0)
        side = get(tile)
        turn = (4 - before - start) % ROWS
        side = pltpu.roll(side, turn, 0) if turn else side
        head = jnp.where(half >= 4, main, jnp.where(half >= 4 - before, side, 0.0))
        tail = jnp.where(half < 4, main, jnp.where(half < 4 + after, side, 0.0))
        return jnp.concatenate([head, tail])

    def below(k):
        return jnp.where(low, far[k], near[k])

    def above(k):
        return jnp.where(low, near[k], far[k])

    sources = {
        -2: lambda k: below(PLANE + k),
        -1: below,
        0: lambda k: mine[1 - core, k],
        1: lambda k: mine[core, k],
        2: above,
        3: lambda k: above(PLANE + k),
    }
    couplings = ("z", "zy", "zx", "y", "x", "yx")
    coefs = {}
    for p in range(-1, 4):
        names = couplings[:3] if p == 3 else couplings
        coefs[p] = {n: (spread(sources[p], n + "r"), spread(sources[p], n + "i")) for n in names}
        if p < 3:
            coefs[p]["d"] = spread(sources[p], "d") + DAMPING
    v0 = {p: (spread(sources[p], "rr"), spread(sources[p], "ri")) for p in range(-2, 4)}

    def mul(c, m):
        return c[0] * m[0] - c[1] * m[1], c[0] * m[1] + c[1] * m[0]

    def conj(c, m):
        return c[0] * m[0] + c[1] * m[1], c[0] * m[1] - c[1] * m[0]

    def plus(*terms):
        return tuple(functools.reduce(lambda a, b: a + b, part) for part in zip(*terms))

    def ahead_y(x):
        return pltpu.roll(x, 2 * ROWS - 1, 0)

    def behind_y(x):
        return pltpu.roll(x, 1, 0)

    def apply(field, planes):
        stepped = {}
        flat = {}
        for p in planes + [planes[-1] + 1]:
            c, m = coefs[p], field[p]
            back = field.get(p - 1)
            my = tuple(behind_y(v) for v in m)
            mx = tuple(prv(v, 1) for v in m)
            stepped[p] = plus(conj(c["z"], m), mul(c["zy"], my), mul(c["zx"], mx))
            if p > planes[-1]:
                continue
            ys = plus(conj(c["y"], m), conj(c["zy"], back), mul(c["yx"], mx))
            xs = plus(conj(c["x"], m), conj(c["zx"], back), conj(c["yx"], my))
            flat[p] = plus(
                tuple(c["d"] * v for v in m),
                mul(c["z"], back),
                mul(c["y"], my),
                mul(c["x"], mx),
                tuple(ahead_y(v) for v in ys),
                tuple(nxt(v, 1) for v in xs),
            )
        return {p: plus(flat[p], stepped[p + 1]) for p in planes}

    v1 = apply(v0, [-1, 0, 1, 2])
    v2 = apply(v1, [0, 1])

    def own(x):
        return jnp.where(half < 4, pltpu.roll(x[:ROWS], 4, 0), pltpu.roll(x[ROWS:], 4, 0))

    held = [[[own(v[p][part]) for p in range(2)] for part in range(2)] for v in (v0, v1, v2)]
    note = jnp.zeros((ROWS, nx), jnp.float32)
    for k, (a, b) in enumerate(((0, 0), (0, 1), (1, 1), (1, 2))):
        total = sum(held[a][part][p] * held[b][part][p] for part in range(2) for p in range(2))
        note = jnp.where(half == k, jnp.sum(total, axis=0, keepdims=True), note)
    tiles = [tile for vector in held for parts in vector for tile in parts] + [note]
    for k, tile in enumerate(tiles):
        for chip in range(out.shape[0]):
            out[chip, k] = tile


def outputs_kernel(place, sums, gathered, others, modulus, residual):
    core = place[0]
    chips = gathered.shape[0]
    total = sums[0]
    for k in range(1, sums.shape[0]):
        total = total + sums[k]
    total = jnp.broadcast_to(jnp.sum(total, axis=1, keepdims=True), total.shape)
    m0, m1, m2, m3 = (total[k : k + 1] for k in range(4))
    step = m0 / m1
    norm = step * step * m2 - m0
    grown = 1.0 + norm / m0
    curve = grown * grown * m1 - 2.0 * step * grown * m2 + step * step * m3
    second = norm / curve
    shape = (chips, ROWS, total.shape[-1])
    p = jnp.broadcast_to((step + second * grown).reshape(1, 1, -1), shape)
    q = jnp.broadcast_to((step * second).reshape(1, 1, -1), shape)
    for source, first in ((gathered, 2 * core), (others, 2 - 2 * core)):
        for part in range(2):
            for plane in range(2):
                v0, v1, v2 = (source[:, 4 * k + 2 * part + plane] for k in range(3))
                flat = (chips * ROWS, shape[-1])
                modulus[part, first + plane] = (p * v0 - q * v1).reshape(flat)
                residual[part, first + plane] = (v0 - p * v1 + q * v2).reshape(flat)


def run(kernel, shapes, *arrays, scratch=(), scalars=1):
    vmem = pl.BlockSpec(memory_space=pltpu.VMEM)
    smem = pl.BlockSpec(memory_space=pltpu.SMEM)
    return pl.pallas_call(
        kernel,
        out_shape=shapes,
        in_specs=[smem] * scalars + [vmem] * (len(arrays) - scalars),
        out_specs=jax.tree.map(lambda _: vmem, shapes),
        scratch_shapes=list(scratch),
        compiler_params=pltpu.CompilerParams(vmem_limit_bytes=VMEM_BYTES),
    )(*arrays)


def body(displacement, freq_index, tissue):
    core = lax.axis_index("freq") % 2
    chips = lax.axis_size("freq") // 2
    slabs = lax.axis_size("gz")
    low = core == 0
    ny, nx = displacement.shape[-2:]
    tile = (ROWS, nx)
    place = jnp.stack([core, (low & (lax.axis_index("gz") == 0)).astype(jnp.int32)])

    def shape(*dims):
        return jax.ShapeDtypeStruct(dims, jnp.float32)

    field = displacement[0]
    first, last = (field[:, :, k].reshape(6, ny, nx) for k in (0, 3))
    same = to_slabs(jnp.where(low, last, first), 0, 0)
    cross = to_slabs(jnp.concatenate([jnp.where(low, first, last), tissue[:1].astype(jnp.float32)]), 1, 1)
    other = swap_cores(displacement)[0]
    other_index = swap_cores(freq_index)

    held = (place, freq_index, other_index, field, other, tissue)
    scratch = [pltpu.VMEM((15, ny + 2 * ROWS, nx), jnp.float32)]
    inner = run(inner_kernel, shape(chips, PLANE, *tile), *held, scratch=scratch, scalars=3)
    parts = run(outer_kernel, shape(chips, 2 * PLANE, *tile), *held, same, cross, inner, scratch=scratch, scalars=3)
    mine = over_chips(parts).sum(axis=0).reshape(2, PLANE, *tile)

    near = swap_cores(jnp.concatenate([mine[0], mine[1, :BEYOND]]))
    far = to_slabs(jnp.concatenate([mine[1], mine[0, :BEYOND]]), 1, 1)
    tiles = run(vectors_kernel, shape(chips, 13, *tile), place, mine, near, far)

    gathered = over_chips(tiles)
    others = swap_cores(gathered)
    members = [[(2 * chip + core) * slabs + g for core in range(2) for g in range(slabs)] for chip in range(chips)]
    sums = jnp.broadcast_to(gathered[:, 12].sum(axis=0), (2 * slabs, *tile))
    sums = lax.all_to_all(sums, ("freq", "gz"), split_axis=0, concat_axis=0, tiled=True, axis_index_groups=members)
    result = shape(2, 4, ny, nx)
    return tuple(run(outputs_kernel, (result, result), place, sums, gathered, others))


def solution(mesh):
    placed = (P("freq", None, None, "gz", None, None), P("freq"), P("gz", None, None))
    return jax.shard_map(
        body,
        mesh=mesh,
        in_specs=placed,
        out_specs=(P(None, "gz", None, None), P(None, "gz", None, None)),
        check_vma=False,
    )
```

```python
import functools

import jax
import jax.numpy as jnp
from jax import lax
from jax.experimental import pallas as pl
from jax.experimental.pallas import tpu as pltpu
from jax.sharding import PartitionSpec as P

DAMPING = 0.05
ROWS = 8
VMEM_BYTES = 12 << 20

NAMES = ("zr", "zi", "zyr", "zyi", "zxr", "zxi", "rr", "ri", None, None, None, "d", "yr", "yi", "xr", "xi", "yxr", "yxi", None, None)
MAIN = {name: k for k, name in enumerate(NAMES) if name}
AROUND = {
    8: (("zyr", 0, 1, 2), ("zyi", 3, 1, 2), ("zr", 6, 1, 1)),
    9: (("zi", 0, 1, 1), ("zxr", 2, 1, 1), ("zxi", 4, 1, 1), ("xi", 6, 1, 1)),
    10: (("rr", 0, 2, 2), ("ri", 4, 2, 2)),
    18: (("yr", 0, 1, 2), ("yi", 3, 1, 2), ("d", 6, 1, 1)),
    19: (("yxr", 0, 1, 2), ("yxi", 3, 1, 2), ("xr", 6, 1, 1)),
}
PLANE = len(NAMES)
BEYOND = 11


def swap_cores(array):
    pairs = [(i, i ^ 1) for i in range(lax.axis_size("freq"))]
    return lax.ppermute(array, "freq", pairs)


def to_slabs(array, first_up, cross):
    peers, slabs = lax.axis_size("freq"), lax.axis_size("gz")
    pairs = []
    for f in range(peers):
        for g in range(slabs):
            to = g + 1 if f % 2 == first_up else g - 1
            if 0 <= to < slabs:
                pairs.append((f * slabs + g, (f ^ cross) * slabs + to))
    return lax.ppermute(array, ("freq", "gz"), pairs)


def over_chips(parts):
    peers = lax.axis_size("freq")
    groups = [list(range(core, peers, 2)) for core in range(2)]
    return lax.all_to_all(parts, "freq", split_axis=0, concat_axis=0, tiled=True, axis_index_groups=groups)


def rows_of(shape, dim):
    return lax.broadcasted_iota(jnp.int32, shape, dim)


def nxt(x, dim):
    size = x.shape[dim]
    return jnp.where(rows_of(x.shape, dim) == size - 1, 0.0, pltpu.roll(x, size - 1, dim))


def prv(x, dim):
    return jnp.where(rows_of(x.shape, dim) == 0, 0.0, pltpu.roll(x, 1, dim))


def products(cell, kappas, masks, out, first, rows):
    nx = out.shape[-1]
    ny = out.shape[0] * ROWS
    tile = (ROWS, nx)
    line, lane = rows_of(tile, 0), rows_of(tile, 1)
    blank = jnp.zeros(tile, jnp.float32)

    def at(read, j):
        return read(pl.ds(ROWS * j, ROWS))

    def next_y(read, j):
        if ROWS * j + ROWS < ny:
            return read(pl.ds(ROWS * j + 1, ROWS))
        return jnp.where(line == ROWS - 1, 0.0, pltpu.roll(at(read, j), ROWS - 1, 0))

    def prev_y(read, j):
        if j:
            return read(pl.ds(ROWS * j - 1, ROWS))
        return pltpu.roll(at(read, j), 1, 0)

    def re(a, b):
        return a[0] * b[0] + a[1] * b[1]

    def im(a, b):
        return a[0] * b[1] - a[1] * b[0]

    names = [name for name in NAMES if name]
    for k in range(len(names)):
        rows[k, :ROWS] = blank
        rows[k, ROWS + ny :] = blank
    for j in range(ny // ROWS):
        here, above = (at(mask, j) for mask in masks)
        here_y, here_x = next_y(masks[0], j), nxt(here, 1)
        sums = None
        for group in range(2):
            scales = [m * kappas[group] for m in (here, above, here_y, here_x)]
            for comp in range(3):
                gz, gp, gy, gx, hy, hx, s, t = ([] for _ in range(8))
                for part in range(2):
                    below, mine, up = cell(group, part, comp)
                    u, uz = at(mine, j), at(up, j)
                    uy, ux = next_y(mine, j), nxt(u, 1)
                    gz.append(uz - u)
                    gp.append(u - at(below, j))
                    gy.append(uy - u)
                    gx.append(ux - u)
                    step = u - prev_y(mine, j)
                    hy.append(step if j else jnp.where(line == 0, 0.0, step))
                    hx.append(jnp.where(lane == 0, 0.0, u - pltpu.roll(u, 1, 1)))
                    s.append(gz[-1] + gy[-1] + gx[-1])
                    t.append([u * scales[0], uz * scales[1], uy * scales[2], ux * scales[3]])
                new = [re(s, s), re(gz, gz), re(gy, gy), re(gx, gx)]
                for a, b in ((s, gp), (s, hy), (s, hx), (gp, hy), (gp, hx), (hy, hx)):
                    new += [re(a, b), im(a, b)]
                ts = [[t[0][k], t[1][k]] for k in range(4)]
                for f in (re, im):
                    new.append(f(gz, ts[1]) + f(gy, ts[2]) + f(gx, ts[3]) - f(s, ts[0]))
                sums = new if sums is None else [old + value for old, value in zip(sums, new)]
        done = {"d": here * sums[0] + above * sums[1] + here_y * sums[2] + here_x * sums[3]}
        for k, name in enumerate(("z", "y", "x", "zy", "zx", "yx")):
            signed = -here if k < 3 else here
            done[name + "r"] = signed * sums[4 + 2 * k]
            done[name + "i"] = signed * sums[5 + 2 * k]
        done["rr"], done["ri"] = sums[16], sums[17]
        for k, name in enumerate(names):
            out[j, first + MAIN[name]] = done[name]
            rows[k, ROWS + ROWS * j : 2 * ROWS + ROWS * j] = done[name]
    for j in range(ny // ROWS):
        for k, parts in AROUND.items():
            packed = blank
            for name, start, before, after in parts:
                kept = names.index(name)
                middle = start + before
                head = rows[kept, pl.ds(ROWS + ROWS * j - middle, ROWS)]
                tail = rows[kept, pl.ds(2 * ROWS + ROWS * j - middle, ROWS)]
                packed = jnp.where((line >= start) & (line < middle), head, packed)
                packed = jnp.where((line >= middle) & (line < middle + after), tail, packed)
            out[j, first + k] = packed


def kappa_of(index):
    return 0.2 * (index[0] + 1).astype(jnp.float32)


def inner_kernel(place, index, other_index, field, other, tissue, out, rows):
    core = place[0]

    def cell(group, part, comp):
        source = field if group == 0 else other
        return [lambda at, k=k: source[part, comp, core + k, at] for k in range(3)]

    masks = [lambda at, k=k: tissue[core + k, at].astype(jnp.float32) for k in (1, 2)]
    products(cell, (kappa_of(index), kappa_of(other_index)), masks, out, 0, rows)


def outer_kernel(place, index, other_index, field, other, tissue, same, cross, inner, out, rows):
    core = place[0]
    low, floor = core == 0, place[1] == 1
    out[:, :PLANE] = inner[...]

    def cell(group, part, comp):
        source = field if group == 0 else other

        def outside(at):
            return (same, cross)[group][3 * part + comp, at]

        def mine(at):
            return source[part, comp, 3 * core, at]

        def inside(at):
            return source[part, comp, 1 + core, at]

        def below(at):
            return jnp.where(low, jnp.where(floor, mine(at), outside(at)), inside(at))

        return below, mine, lambda at: jnp.where(low, inside(at), outside(at))

    def here(at):
        return tissue[3 * core, at].astype(jnp.float32)

    def above(at):
        return jnp.where(low, tissue[1, at].astype(jnp.float32), cross[6, at])

    products(cell, (kappa_of(index), kappa_of(other_index)), (here, above), out, PLANE, rows)


def around_of(name):
    for tile, parts in AROUND.items():
        for other, start, before, after in parts:
            if other == name:
                return tile, start, before, after
    raise KeyError(name)


def vectors_kernel(place, mine, near, far, out):
    core = place[0]
    low = core == 0
    nx = mine.shape[-1]
    half = rows_of((ROWS, nx), 0)

    def spread(get, name):
        tile, start, before, after = around_of(name)
        main = pltpu.roll(get(MAIN[name]), 4, 0)
        side = get(tile)
        turn = (4 - before - start) % ROWS
        side = pltpu.roll(side, turn, 0) if turn else side
        head = jnp.where(half >= 4, main, jnp.where(half >= 4 - before, side, 0.0))
        tail = jnp.where(half < 4, main, jnp.where(half < 4 + after, side, 0.0))
        return jnp.concatenate([head, tail])

    def below(k):
        return jnp.where(low, far[k], near[k])

    def above(k):
        return jnp.where(low, near[k], far[k])

    sources = {
        -2: lambda k: below(PLANE + k),
        -1: below,
        0: lambda k: mine[1 - core, k],
        1: lambda k: mine[core, k],
        2: above,
        3: lambda k: above(PLANE + k),
    }
    couplings = ("z", "zy", "zx", "y", "x", "yx")
    coefs = {}
    for p in range(-1, 4):
        names = couplings[:3] if p == 3 else couplings
        coefs[p] = {n: (spread(sources[p], n + "r"), spread(sources[p], n + "i")) for n in names}
        if p < 3:
            coefs[p]["d"] = spread(sources[p], "d") + DAMPING
    v0 = {p: (spread(sources[p], "rr"), spread(sources[p], "ri")) for p in range(-2, 4)}

    def mul(c, m):
        return c[0] * m[0] - c[1] * m[1], c[0] * m[1] + c[1] * m[0]

    def conj(c, m):
        return c[0] * m[0] + c[1] * m[1], c[0] * m[1] - c[1] * m[0]

    def plus(*terms):
        return tuple(functools.reduce(lambda a, b: a + b, part) for part in zip(*terms))

    def ahead_y(x):
        return pltpu.roll(x, 2 * ROWS - 1, 0)

    def behind_y(x):
        return pltpu.roll(x, 1, 0)

    def apply(field, planes):
        stepped = {}
        flat = {}
        for p in planes + [planes[-1] + 1]:
            c, m = coefs[p], field[p]
            back = field.get(p - 1)
            my = tuple(behind_y(v) for v in m)
            mx = tuple(prv(v, 1) for v in m)
            stepped[p] = plus(conj(c["z"], m), mul(c["zy"], my), mul(c["zx"], mx))
            if p > planes[-1]:
                continue
            ys = plus(conj(c["y"], m), conj(c["zy"], back), mul(c["yx"], mx))
            xs = plus(conj(c["x"], m), conj(c["zx"], back), conj(c["yx"], my))
            flat[p] = plus(
                tuple(c["d"] * v for v in m),
                mul(c["z"], back),
                mul(c["y"], my),
                mul(c["x"], mx),
                tuple(ahead_y(v) for v in ys),
                tuple(nxt(v, 1) for v in xs),
            )
        return {p: plus(flat[p], stepped[p + 1]) for p in planes}

    v1 = apply(v0, [-1, 0, 1, 2])
    v2 = apply(v1, [0, 1])

    def own(x):
        return jnp.where(half < 4, pltpu.roll(x[:ROWS], 4, 0), pltpu.roll(x[ROWS:], 4, 0))

    held = [[[own(v[p][part]) for p in range(2)] for part in range(2)] for v in (v0, v1, v2)]
    note = jnp.zeros((ROWS, nx), jnp.float32)
    for k, (a, b) in enumerate(((0, 0), (0, 1), (1, 1), (1, 2))):
        total = sum(held[a][part][p] * held[b][part][p] for part in range(2) for p in range(2))
        note = jnp.where(half == k, jnp.sum(total, axis=0, keepdims=True), note)
    tiles = [tile for vector in held for parts in vector for tile in parts] + [note]
    for k, tile in enumerate(tiles):
        for chip in range(out.shape[0]):
            out[chip, k] = tile


def outputs_kernel(place, sums, gathered, others, modulus, residual, held, sems):
    core = place[0]
    chips = gathered.shape[0]
    total = sums[0]
    for k in range(1, sums.shape[0]):
        total = total + sums[k]
    total = jnp.broadcast_to(jnp.sum(total, axis=1, keepdims=True), total.shape)
    m0, m1, m2, m3 = (total[k : k + 1] for k in range(4))
    step = m0 / m1
    norm = step * step * m2 - m0
    grown = 1.0 + norm / m0
    curve = grown * grown * m1 - 2.0 * step * grown * m2 + step * step * m3
    second = norm / curve
    shape = (chips, ROWS, total.shape[-1])
    p = jnp.broadcast_to((step + second * grown).reshape(1, 1, -1), shape)
    q = jnp.broadcast_to((step * second).reshape(1, 1, -1), shape)
    copies = []
    for source, first in ((gathered, 2 * core), (others, 2 - 2 * core)):
        for part in range(2):
            for plane in range(2):
                v0, v1, v2 = (source[:, 4 * k + 2 * part + plane] for k in range(3))
                flat = (chips * ROWS, shape[-1])
                for out, value in ((modulus, p * v0 - q * v1), (residual, v0 - p * v1 + q * v2)):
                    slot = len(copies)
                    held[slot] = value.reshape(flat)
                    copies.append(pltpu.make_async_copy(held.at[slot], out.at[part, first + plane], sems.at[slot]))
                    copies[-1].start()
    for copy in copies:
        copy.wait()


def run(kernel, shapes, *arrays, scratch=(), scalars=1, outs=None):
    vmem = pl.BlockSpec(memory_space=pltpu.VMEM)
    smem = pl.BlockSpec(memory_space=pltpu.SMEM)
    return pl.pallas_call(
        kernel,
        out_shape=shapes,
        in_specs=[smem] * scalars + [vmem] * (len(arrays) - scalars),
        out_specs=jax.tree.map(lambda _: outs or vmem, shapes),
        scratch_shapes=list(scratch),
        compiler_params=pltpu.CompilerParams(vmem_limit_bytes=VMEM_BYTES),
    )(*arrays)


def body(displacement, freq_index, tissue):
    core = lax.axis_index("freq") % 2
    chips = lax.axis_size("freq") // 2
    slabs = lax.axis_size("gz")
    low = core == 0
    ny, nx = displacement.shape[-2:]
    tile = (ROWS, nx)
    place = jnp.stack([core, (low & (lax.axis_index("gz") == 0)).astype(jnp.int32)])

    def shape(*dims):
        return jax.ShapeDtypeStruct(dims, jnp.float32)

    other = swap_cores(displacement)[0]
    other_index = swap_cores(freq_index)
    displacement, tissue, other_index = lax.optimization_barrier((displacement, tissue, other_index))
    field = displacement[0]
    first, last = (field[:, :, k].reshape(6, ny, nx) for k in (0, 3))
    same = to_slabs(jnp.where(low, last, first), 0, 0)
    cross = to_slabs(jnp.concatenate([jnp.where(low, first, last), tissue[:1].astype(jnp.float32)]), 1, 1)

    held = (place, freq_index, other_index, field, other, tissue)
    scratch = [pltpu.VMEM((15, ny + 2 * ROWS, nx), jnp.float32)]
    inner = run(inner_kernel, shape(chips, PLANE, *tile), *held, scratch=scratch, scalars=3)
    parts = run(outer_kernel, shape(chips, 2 * PLANE, *tile), *held, same, cross, inner, scratch=scratch, scalars=3)
    mine = over_chips(parts).sum(axis=0).reshape(2, PLANE, *tile)

    near = swap_cores(jnp.concatenate([mine[0], mine[1, :BEYOND]]))
    far = to_slabs(jnp.concatenate([mine[1], mine[0, :BEYOND]]), 1, 1)
    tiles = run(vectors_kernel, shape(chips, 13, *tile), place, mine, near, far)

    gathered = over_chips(tiles)
    sums = gathered[:, 12].sum(axis=0)
    sums, gathered = lax.optimization_barrier((sums + swap_cores(sums), gathered))
    others = swap_cores(gathered)
    sums = lax.all_to_all(jnp.broadcast_to(sums, (slabs, *tile)), "gz", split_axis=0, concat_axis=0, tiled=True)
    result = shape(2, 4, ny, nx)
    scratch = [pltpu.VMEM((16, ny, nx), jnp.float32), pltpu.SemaphoreType.DMA((16,))]
    outs = pl.BlockSpec(memory_space=pl.ANY)
    return tuple(run(outputs_kernel, (result, result), place, sums, gathered, others, scratch=scratch, outs=outs))


def solution(mesh):
    placed = (P("freq", None, None, "gz", None, None), P("freq"), P("gz", None, None))
    return jax.shard_map(
        body,
        mesh=mesh,
        in_specs=placed,
        out_specs=(P(None, "gz", None, None), P(None, "gz", None, None)),
        check_vma=False,
    )
```

```python
import functools

import jax
import jax.numpy as jnp
from jax import lax
from jax.experimental import pallas as pl
from jax.experimental.pallas import tpu as pltpu
from jax.sharding import PartitionSpec as P

DAMPING = 0.05
ROWS = 8
VMEM_BYTES = 12 << 20

NAMES = ("zr", "zi", "zyr", "zyi", "zxr", "zxi", "rr", "ri", None, None, None, "d", "yr", "yi", "xr", "xi", "yxr", "yxi", None, None)
MAIN = {name: k for k, name in enumerate(NAMES) if name}
AROUND = {
    8: (("zyr", 0, 1, 2), ("zyi", 3, 1, 2), ("zr", 6, 1, 1)),
    9: (("zi", 0, 1, 1), ("zxr", 2, 1, 1), ("zxi", 4, 1, 1), ("xi", 6, 1, 1)),
    10: (("rr", 0, 2, 2), ("ri", 4, 2, 2)),
    18: (("yr", 0, 1, 2), ("yi", 3, 1, 2), ("d", 6, 1, 1)),
    19: (("yxr", 0, 1, 2), ("yxi", 3, 1, 2), ("xr", 6, 1, 1)),
}
PLANE = len(NAMES)
BEYOND = 11


def swap_cores(array):
    pairs = [(i, i ^ 1) for i in range(lax.axis_size("freq"))]
    return lax.ppermute(array, "freq", pairs)


def to_slabs(array, first_up, cross):
    peers, slabs = lax.axis_size("freq"), lax.axis_size("gz")
    pairs = []
    for f in range(peers):
        for g in range(slabs):
            to = g + 1 if f % 2 == first_up else g - 1
            if 0 <= to < slabs:
                pairs.append((f * slabs + g, (f ^ cross) * slabs + to))
    return lax.ppermute(array, ("freq", "gz"), pairs)


def over_chips(parts):
    peers = lax.axis_size("freq")
    groups = [list(range(core, peers, 2)) for core in range(2)]
    return lax.all_to_all(parts, "freq", split_axis=0, concat_axis=0, tiled=True, axis_index_groups=groups)


def rows_of(shape, dim):
    return lax.broadcasted_iota(jnp.int32, shape, dim)


def nxt(x, dim):
    size = x.shape[dim]
    return jnp.where(rows_of(x.shape, dim) == size - 1, 0.0, pltpu.roll(x, size - 1, dim))


def prv(x, dim):
    return jnp.where(rows_of(x.shape, dim) == 0, 0.0, pltpu.roll(x, 1, dim))


def products(cell, kappas, masks, out, first, rows):
    nx = out.shape[-1]
    ny = out.shape[0] * ROWS
    tile = (ROWS, nx)
    line, lane = rows_of(tile, 0), rows_of(tile, 1)
    blank = jnp.zeros(tile, jnp.float32)

    def at(read, j):
        return read(pl.ds(ROWS * j, ROWS))

    def next_y(read, j):
        if ROWS * j + ROWS < ny:
            return read(pl.ds(ROWS * j + 1, ROWS))
        return jnp.where(line == ROWS - 1, 0.0, pltpu.roll(at(read, j), ROWS - 1, 0))

    def prev_y(read, j):
        if j:
            return read(pl.ds(ROWS * j - 1, ROWS))
        return pltpu.roll(at(read, j), 1, 0)

    def re(a, b):
        return a[0] * b[0] + a[1] * b[1]

    def im(a, b):
        return a[0] * b[1] - a[1] * b[0]

    names = [name for name in NAMES if name]
    for k in range(len(names)):
        rows[k, :ROWS] = blank
        rows[k, ROWS + ny :] = blank
    for j in range(ny // ROWS):
        here, above = (at(mask, j) for mask in masks)
        here_y, here_x = next_y(masks[0], j), nxt(here, 1)
        sums = None
        for group in range(2):
            scales = [m * kappas[group] for m in (here, above, here_y, here_x)]
            for comp in range(3):
                gz, gp, gy, gx, hy, hx, s, t = ([] for _ in range(8))
                for part in range(2):
                    below, mine, up = cell(group, part, comp)
                    u, uz = at(mine, j), at(up, j)
                    uy, ux = next_y(mine, j), nxt(u, 1)
                    gz.append(uz - u)
                    gp.append(u - at(below, j))
                    gy.append(uy - u)
                    gx.append(ux - u)
                    step = u - prev_y(mine, j)
                    hy.append(step if j else jnp.where(line == 0, 0.0, step))
                    hx.append(jnp.where(lane == 0, 0.0, u - pltpu.roll(u, 1, 1)))
                    s.append(gz[-1] + gy[-1] + gx[-1])
                    t.append([u * scales[0], uz * scales[1], uy * scales[2], ux * scales[3]])
                new = [re(s, s), re(gz, gz), re(gy, gy), re(gx, gx)]
                for a, b in ((s, gp), (s, hy), (s, hx), (gp, hy), (gp, hx), (hy, hx)):
                    new += [re(a, b), im(a, b)]
                ts = [[t[0][k], t[1][k]] for k in range(4)]
                for f in (re, im):
                    new.append(f(gz, ts[1]) + f(gy, ts[2]) + f(gx, ts[3]) - f(s, ts[0]))
                sums = new if sums is None else [old + value for old, value in zip(sums, new)]
        done = {"d": here * sums[0] + above * sums[1] + here_y * sums[2] + here_x * sums[3]}
        for k, name in enumerate(("z", "y", "x", "zy", "zx", "yx")):
            signed = -here if k < 3 else here
            done[name + "r"] = signed * sums[4 + 2 * k]
            done[name + "i"] = signed * sums[5 + 2 * k]
        done["rr"], done["ri"] = sums[16], sums[17]
        for k, name in enumerate(names):
            out[j, first + MAIN[name]] = done[name]
            rows[k, ROWS + ROWS * j : 2 * ROWS + ROWS * j] = done[name]
    for j in range(ny // ROWS):
        for k, parts in AROUND.items():
            packed = blank
            for name, start, before, after in parts:
                kept = names.index(name)
                middle = start + before
                head = rows[kept, pl.ds(ROWS + ROWS * j - middle, ROWS)]
                tail = rows[kept, pl.ds(2 * ROWS + ROWS * j - middle, ROWS)]
                packed = jnp.where((line >= start) & (line < middle), head, packed)
                packed = jnp.where((line >= middle) & (line < middle + after), tail, packed)
            out[j, first + k] = packed


def kappa_of(index):
    return 0.2 * (index[0] + 1).astype(jnp.float32)


def inner_kernel(place, index, other_index, field, other, tissue, out, rows):
    core = place[0]

    def cell(group, part, comp):
        source = field if group == 0 else other
        return [lambda at, k=k: source[part, comp, core + k, at] for k in range(3)]

    masks = [lambda at, k=k: tissue[core + k, at].astype(jnp.float32) for k in (1, 2)]
    products(cell, (kappa_of(index), kappa_of(other_index)), masks, out, 0, rows)


def outer_kernel(place, index, other_index, field, other, tissue, same, cross, inner, out, rows):
    core = place[0]
    low, floor = core == 0, place[1] == 1
    out[:, :PLANE] = inner[...]

    def cell(group, part, comp):
        source = field if group == 0 else other

        def outside(at):
            return (same, cross)[group][3 * part + comp, at]

        def mine(at):
            return source[part, comp, 3 * core, at]

        def inside(at):
            return source[part, comp, 1 + core, at]

        def below(at):
            return jnp.where(low, jnp.where(floor, mine(at), outside(at)), inside(at))

        return below, mine, lambda at: jnp.where(low, inside(at), outside(at))

    def here(at):
        return tissue[3 * core, at].astype(jnp.float32)

    def above(at):
        return jnp.where(low, tissue[1, at].astype(jnp.float32), cross[6, at])

    products(cell, (kappa_of(index), kappa_of(other_index)), (here, above), out, PLANE, rows)


def around_of(name):
    for tile, parts in AROUND.items():
        for other, start, before, after in parts:
            if other == name:
                return tile, start, before, after
    raise KeyError(name)


def vectors_kernel(place, mine, near, far, out):
    core = place[0]
    low = core == 0
    nx = mine.shape[-1]
    half = rows_of((ROWS, nx), 0)

    def spread(get, name):
        tile, start, before, after = around_of(name)
        main = pltpu.roll(get(MAIN[name]), 4, 0)
        side = get(tile)
        turn = (4 - before - start) % ROWS
        side = pltpu.roll(side, turn, 0) if turn else side
        head = jnp.where(half >= 4, main, jnp.where(half >= 4 - before, side, 0.0))
        tail = jnp.where(half < 4, main, jnp.where(half < 4 + after, side, 0.0))
        return jnp.concatenate([head, tail])

    def below(k):
        return jnp.where(low, far[k], near[k])

    def above(k):
        return jnp.where(low, near[k], far[k])

    sources = {
        -2: lambda k: below(PLANE + k),
        -1: below,
        0: lambda k: mine[1 - core, k],
        1: lambda k: mine[core, k],
        2: above,
        3: lambda k: above(PLANE + k),
    }
    couplings = ("z", "zy", "zx", "y", "x", "yx")
    coefs = {}
    for p in range(-1, 4):
        names = couplings[:3] if p == 3 else couplings
        coefs[p] = {n: (spread(sources[p], n + "r"), spread(sources[p], n + "i")) for n in names}
        if p < 3:
            coefs[p]["d"] = spread(sources[p], "d") + DAMPING
    v0 = {p: (spread(sources[p], "rr"), spread(sources[p], "ri")) for p in range(-2, 4)}

    def mul(c, m):
        return c[0] * m[0] - c[1] * m[1], c[0] * m[1] + c[1] * m[0]

    def conj(c, m):
        return c[0] * m[0] + c[1] * m[1], c[0] * m[1] - c[1] * m[0]

    def plus(*terms):
        return tuple(functools.reduce(lambda a, b: a + b, part) for part in zip(*terms))

    def ahead_y(x):
        return pltpu.roll(x, 2 * ROWS - 1, 0)

    def behind_y(x):
        return pltpu.roll(x, 1, 0)

    def apply(field, planes):
        stepped = {}
        flat = {}
        for p in planes + [planes[-1] + 1]:
            c, m = coefs[p], field[p]
            back = field.get(p - 1)
            my = tuple(behind_y(v) for v in m)
            mx = tuple(prv(v, 1) for v in m)
            stepped[p] = plus(conj(c["z"], m), mul(c["zy"], my), mul(c["zx"], mx))
            if p > planes[-1]:
                continue
            ys = plus(conj(c["y"], m), conj(c["zy"], back), mul(c["yx"], mx))
            xs = plus(conj(c["x"], m), conj(c["zx"], back), conj(c["yx"], my))
            flat[p] = plus(
                tuple(c["d"] * v for v in m),
                mul(c["z"], back),
                mul(c["y"], my),
                mul(c["x"], mx),
                tuple(ahead_y(v) for v in ys),
                tuple(nxt(v, 1) for v in xs),
            )
        return {p: plus(flat[p], stepped[p + 1]) for p in planes}

    v1 = apply(v0, [-1, 0, 1, 2])
    v2 = apply(v1, [0, 1])

    def own(x):
        return jnp.where(half < 4, pltpu.roll(x[:ROWS], 4, 0), pltpu.roll(x[ROWS:], 4, 0))

    held = [[[own(v[p][part]) for p in range(2)] for part in range(2)] for v in (v0, v1, v2)]
    note = jnp.zeros((ROWS, nx), jnp.float32)
    for k, (a, b) in enumerate(((0, 0), (0, 1), (1, 1), (1, 2))):
        total = sum(held[a][part][p] * held[b][part][p] for part in range(2) for p in range(2))
        note = jnp.where(half == k, jnp.sum(total, axis=0, keepdims=True), note)
    tiles = [tile for vector in held for parts in vector for tile in parts] + [note]
    for k, tile in enumerate(tiles):
        for chip in range(out.shape[0]):
            out[chip, k] = tile


def outputs_kernel(place, sums, gathered, others, modulus, residual):
    core = place[0]
    chips = gathered.shape[0]
    total = sums[0]
    for k in range(1, sums.shape[0]):
        total = total + sums[k]
    total = jnp.broadcast_to(jnp.sum(total, axis=1, keepdims=True), total.shape)
    m0, m1, m2, m3 = (total[k : k + 1] for k in range(4))
    step = m0 / m1
    norm = step * step * m2 - m0
    grown = 1.0 + norm / m0
    curve = grown * grown * m1 - 2.0 * step * grown * m2 + step * step * m3
    second = norm / curve
    shape = (chips, ROWS, total.shape[-1])
    p = jnp.broadcast_to((step + second * grown).reshape(1, 1, -1), shape)
    q = jnp.broadcast_to((step * second).reshape(1, 1, -1), shape)
    for source, first in ((gathered, 2 * core), (others, 2 - 2 * core)):
        for part in range(2):
            for plane in range(2):
                v0, v1, v2 = (source[:, 4 * k + 2 * part + plane] for k in range(3))
                flat = (chips * ROWS, shape[-1])
                modulus[part, first + plane] = (p * v0 - q * v1).reshape(flat)
                residual[part, first + plane] = (v0 - p * v1 + q * v2).reshape(flat)


def run(kernel, shapes, *arrays, scratch=(), scalars=1):
    vmem = pl.BlockSpec(memory_space=pltpu.VMEM)
    smem = pl.BlockSpec(memory_space=pltpu.SMEM)
    return pl.pallas_call(
        kernel,
        out_shape=shapes,
        in_specs=[smem] * scalars + [vmem] * (len(arrays) - scalars),
        out_specs=jax.tree.map(lambda _: vmem, shapes),
        scratch_shapes=list(scratch),
        compiler_params=pltpu.CompilerParams(vmem_limit_bytes=VMEM_BYTES),
    )(*arrays)


def body(displacement, freq_index, tissue):
    core = lax.axis_index("freq") % 2
    chips = lax.axis_size("freq") // 2
    slabs = lax.axis_size("gz")
    low = core == 0
    ny, nx = displacement.shape[-2:]
    tile = (ROWS, nx)
    place = jnp.stack([core, (low & (lax.axis_index("gz") == 0)).astype(jnp.int32)])

    def shape(*dims):
        return jax.ShapeDtypeStruct(dims, jnp.float32)

    field = displacement[0]
    first, last = (field[:, :, k].reshape(6, ny, nx) for k in (0, 3))
    other = swap_cores(displacement)[0]
    other_index = swap_cores(freq_index)
    same = jnp.where(low, last, first)
    cross = jnp.concatenate([jnp.where(low, first, last), tissue[:1].astype(jnp.float32)])
    same, cross, other_index = lax.optimization_barrier((same, cross, other_index))
    same, cross = to_slabs(same, 0, 0), to_slabs(cross, 1, 1)

    held = (place, freq_index, other_index, field, other, tissue)
    scratch = [pltpu.VMEM((15, ny + 2 * ROWS, nx), jnp.float32)]
    inner = run(inner_kernel, shape(chips, PLANE, *tile), *held, scratch=scratch, scalars=3)
    parts = run(outer_kernel, shape(chips, 2 * PLANE, *tile), *held, same, cross, inner, scratch=scratch, scalars=3)
    mine = over_chips(parts).sum(axis=0).reshape(2, PLANE, *tile)

    near = swap_cores(jnp.concatenate([mine[0], mine[1, :BEYOND]]))
    far = to_slabs(jnp.concatenate([mine[1], mine[0, :BEYOND]]), 1, 1)
    tiles = run(vectors_kernel, shape(chips, 13, *tile), place, mine, near, far)

    gathered = over_chips(tiles)
    sums = gathered[:, 12].sum(axis=0)
    sums, gathered = lax.optimization_barrier((sums + swap_cores(sums), gathered))
    others = swap_cores(gathered)
    sums = lax.all_to_all(jnp.broadcast_to(sums, (slabs, *tile)), "gz", split_axis=0, concat_axis=0, tiled=True)
    result = shape(2, 4, ny, nx)
    return tuple(run(outputs_kernel, (result, result), place, sums, gathered, others))


def solution(mesh):
    placed = (P("freq", None, None, "gz", None, None), P("freq"), P("gz", None, None))
    return jax.shard_map(
        body,
        mesh=mesh,
        in_specs=placed,
        out_specs=(P(None, "gz", None, None), P(None, "gz", None, None)),
        check_vma=False,
    )
```

```python
import functools

import jax
import jax.numpy as jnp
from jax import lax
from jax.experimental import pallas as pl
from jax.experimental.pallas import tpu as pltpu
from jax.sharding import PartitionSpec as P

DAMPING = 0.05
ROWS = 8
VMEM_BYTES = 12 << 20

NAMES = ("zr", "zi", "zyr", "zyi", "zxr", "zxi", "rr", "ri", None, None, None, "d", "yr", "yi", "xr", "xi", "yxr", "yxi", None, None)
MAIN = {name: k for k, name in enumerate(NAMES) if name}
AROUND = {
    8: (("zyr", 0, 1, 2), ("zyi", 3, 1, 2), ("zr", 6, 1, 1)),
    9: (("zi", 0, 1, 1), ("zxr", 2, 1, 1), ("zxi", 4, 1, 1), ("xi", 6, 1, 1)),
    10: (("rr", 0, 2, 2), ("ri", 4, 2, 2)),
    18: (("yr", 0, 1, 2), ("yi", 3, 1, 2), ("d", 6, 1, 1)),
    19: (("yxr", 0, 1, 2), ("yxi", 3, 1, 2), ("xr", 6, 1, 1)),
}
PLANE = len(NAMES)
BEYOND = 11


def swap_cores(array):
    pairs = [(i, i ^ 1) for i in range(lax.axis_size("freq"))]
    return lax.ppermute(array, "freq", pairs)


def to_slabs(array, first_up, cross):
    peers, slabs = lax.axis_size("freq"), lax.axis_size("gz")
    pairs = []
    for f in range(peers):
        for g in range(slabs):
            to = g + 1 if f % 2 == first_up else g - 1
            if 0 <= to < slabs:
                pairs.append((f * slabs + g, (f ^ cross) * slabs + to))
    return lax.ppermute(array, ("freq", "gz"), pairs)


def over_chips(parts):
    peers = lax.axis_size("freq")
    groups = [list(range(core, peers, 2)) for core in range(2)]
    return lax.all_to_all(parts, "freq", split_axis=0, concat_axis=0, tiled=True, axis_index_groups=groups)


def rows_of(shape, dim):
    return lax.broadcasted_iota(jnp.int32, shape, dim)


def nxt(x, dim):
    size = x.shape[dim]
    return jnp.where(rows_of(x.shape, dim) == size - 1, 0.0, pltpu.roll(x, size - 1, dim))


def prv(x, dim):
    return jnp.where(rows_of(x.shape, dim) == 0, 0.0, pltpu.roll(x, 1, dim))


def products(cell, kappas, masks, out, first, rows):
    nx = out.shape[-1]
    ny = out.shape[0] * ROWS
    tile = (ROWS, nx)
    line, lane = rows_of(tile, 0), rows_of(tile, 1)
    blank = jnp.zeros(tile, jnp.float32)

    def at(read, j):
        return read(pl.ds(ROWS * j, ROWS))

    def next_y(read, j):
        if ROWS * j + ROWS < ny:
            return read(pl.ds(ROWS * j + 1, ROWS))
        return jnp.where(line == ROWS - 1, 0.0, pltpu.roll(at(read, j), ROWS - 1, 0))

    def prev_y(read, j):
        if j:
            return read(pl.ds(ROWS * j - 1, ROWS))
        return pltpu.roll(at(read, j), 1, 0)

    def re(a, b):
        return a[0] * b[0] + a[1] * b[1]

    def im(a, b):
        return a[0] * b[1] - a[1] * b[0]

    names = [name for name in NAMES if name]
    for k in range(len(names)):
        rows[k, :ROWS] = blank
        rows[k, ROWS + ny :] = blank
    for j in range(ny // ROWS):
        here, above = (at(mask, j) for mask in masks)
        here_y, here_x = next_y(masks[0], j), nxt(here, 1)
        sums = None
        for group in range(2):
            scales = [m * kappas[group] for m in (here, above, here_y, here_x)]
            for comp in range(3):
                gz, gp, gy, gx, hy, hx, s, t = ([] for _ in range(8))
                for part in range(2):
                    below, mine, up = cell(group, part, comp)
                    u, uz = at(mine, j), at(up, j)
                    uy, ux = next_y(mine, j), nxt(u, 1)
                    gz.append(uz - u)
                    gp.append(u - at(below, j))
                    gy.append(uy - u)
                    gx.append(ux - u)
                    step = u - prev_y(mine, j)
                    hy.append(step if j else jnp.where(line == 0, 0.0, step))
                    hx.append(jnp.where(lane == 0, 0.0, u - pltpu.roll(u, 1, 1)))
                    s.append(gz[-1] + gy[-1] + gx[-1])
                    t.append([u * scales[0], uz * scales[1], uy * scales[2], ux * scales[3]])
                new = [re(s, s), re(gz, gz), re(gy, gy), re(gx, gx)]
                for a, b in ((s, gp), (s, hy), (s, hx), (gp, hy), (gp, hx), (hy, hx)):
                    new += [re(a, b), im(a, b)]
                ts = [[t[0][k], t[1][k]] for k in range(4)]
                for f in (re, im):
                    new.append(f(gz, ts[1]) + f(gy, ts[2]) + f(gx, ts[3]) - f(s, ts[0]))
                sums = new if sums is None else [old + value for old, value in zip(sums, new)]
        done = {"d": here * sums[0] + above * sums[1] + here_y * sums[2] + here_x * sums[3]}
        for k, name in enumerate(("z", "y", "x", "zy", "zx", "yx")):
            signed = -here if k < 3 else here
            done[name + "r"] = signed * sums[4 + 2 * k]
            done[name + "i"] = signed * sums[5 + 2 * k]
        done["rr"], done["ri"] = sums[16], sums[17]
        for k, name in enumerate(names):
            out[j, first + MAIN[name]] = done[name]
            rows[k, ROWS + ROWS * j : 2 * ROWS + ROWS * j] = done[name]
    for j in range(ny // ROWS):
        for k, parts in AROUND.items():
            packed = blank
            for name, start, before, after in parts:
                kept = names.index(name)
                middle = start + before
                head = rows[kept, pl.ds(ROWS + ROWS * j - middle, ROWS)]
                tail = rows[kept, pl.ds(2 * ROWS + ROWS * j - middle, ROWS)]
                packed = jnp.where((line >= start) & (line < middle), head, packed)
                packed = jnp.where((line >= middle) & (line < middle + after), tail, packed)
            out[j, first + k] = packed


def kappa_of(index):
    return 0.2 * (index[0] + 1).astype(jnp.float32)


def inner_kernel(place, index, other_index, field, other, tissue, out, rows):
    core = place[0]

    def cell(group, part, comp):
        source = field if group == 0 else other
        return [lambda at, k=k: source[part, comp, core + k, at] for k in range(3)]

    masks = [lambda at, k=k: tissue[core + k, at].astype(jnp.float32) for k in (1, 2)]
    products(cell, (kappa_of(index), kappa_of(other_index)), masks, out, 0, rows)


def outer_kernel(place, index, other_index, field, other, tissue, same, cross, inner, out, rows):
    core = place[0]
    low, floor = core == 0, place[1] == 1
    out[:, :PLANE] = inner[...]

    def cell(group, part, comp):
        source = field if group == 0 else other

        def outside(at):
            return (same, cross)[group][3 * part + comp, at]

        def mine(at):
            return source[part, comp, 3 * core, at]

        def inside(at):
            return source[part, comp, 1 + core, at]

        def below(at):
            return jnp.where(low, jnp.where(floor, mine(at), outside(at)), inside(at))

        return below, mine, lambda at: jnp.where(low, inside(at), outside(at))

    def here(at):
        return tissue[3 * core, at].astype(jnp.float32)

    def above(at):
        return jnp.where(low, tissue[1, at].astype(jnp.float32), cross[6, at])

    products(cell, (kappa_of(index), kappa_of(other_index)), (here, above), out, PLANE, rows)


def around_of(name):
    for tile, parts in AROUND.items():
        for other, start, before, after in parts:
            if other == name:
                return tile, start, before, after
    raise KeyError(name)


def vectors_kernel(place, mine, near, far, out):
    core = place[0]
    low = core == 0
    nx = mine.shape[-1]
    half = rows_of((ROWS, nx), 0)

    def spread(get, name):
        tile, start, before, after = around_of(name)
        main = pltpu.roll(get(MAIN[name]), 4, 0)
        side = get(tile)
        turn = (4 - before - start) % ROWS
        side = pltpu.roll(side, turn, 0) if turn else side
        head = jnp.where(half >= 4, main, jnp.where(half >= 4 - before, side, 0.0))
        tail = jnp.where(half < 4, main, jnp.where(half < 4 + after, side, 0.0))
        return jnp.concatenate([head, tail])

    def below(k):
        return jnp.where(low, far[k], near[k])

    def above(k):
        return jnp.where(low, near[k], far[k])

    sources = {
        -2: lambda k: below(PLANE + k),
        -1: below,
        0: lambda k: mine[1 - core, k],
        1: lambda k: mine[core, k],
        2: above,
        3: lambda k: above(PLANE + k),
    }
    couplings = ("z", "zy", "zx", "y", "x", "yx")
    coefs = {}
    for p in range(-1, 4):
        names = couplings[:3] if p == 3 else couplings
        coefs[p] = {n: (spread(sources[p], n + "r"), spread(sources[p], n + "i")) for n in names}
        if p < 3:
            coefs[p]["d"] = spread(sources[p], "d") + DAMPING
    v0 = {p: (spread(sources[p], "rr"), spread(sources[p], "ri")) for p in range(-2, 4)}

    def mul(c, m):
        return c[0] * m[0] - c[1] * m[1], c[0] * m[1] + c[1] * m[0]

    def conj(c, m):
        return c[0] * m[0] + c[1] * m[1], c[0] * m[1] - c[1] * m[0]

    def plus(*terms):
        return tuple(functools.reduce(lambda a, b: a + b, part) for part in zip(*terms))

    def ahead_y(x):
        return pltpu.roll(x, 2 * ROWS - 1, 0)

    def behind_y(x):
        return pltpu.roll(x, 1, 0)

    def apply(field, planes):
        stepped = {}
        flat = {}
        for p in planes + [planes[-1] + 1]:
            c, m = coefs[p], field[p]
            back = field.get(p - 1)
            my = tuple(behind_y(v) for v in m)
            mx = tuple(prv(v, 1) for v in m)
            stepped[p] = plus(conj(c["z"], m), mul(c["zy"], my), mul(c["zx"], mx))
            if p > planes[-1]:
                continue
            ys = plus(conj(c["y"], m), conj(c["zy"], back), mul(c["yx"], mx))
            xs = plus(conj(c["x"], m), conj(c["zx"], back), conj(c["yx"], my))
            flat[p] = plus(
                tuple(c["d"] * v for v in m),
                mul(c["z"], back),
                mul(c["y"], my),
                mul(c["x"], mx),
                tuple(ahead_y(v) for v in ys),
                tuple(nxt(v, 1) for v in xs),
            )
        return {p: plus(flat[p], stepped[p + 1]) for p in planes}

    v1 = apply(v0, [-1, 0, 1, 2])
    v2 = apply(v1, [0, 1])

    def own(x):
        return jnp.where(half < 4, pltpu.roll(x[:ROWS], 4, 0), pltpu.roll(x[ROWS:], 4, 0))

    held = [[[own(v[p][part]) for p in range(2)] for part in range(2)] for v in (v0, v1, v2)]
    note = jnp.zeros((ROWS, nx), jnp.float32)
    for k, (a, b) in enumerate(((0, 0), (0, 1), (1, 1), (1, 2))):
        total = sum(held[a][part][p] * held[b][part][p] for part in range(2) for p in range(2))
        note = jnp.where(half == k, jnp.sum(total, axis=0, keepdims=True), note)
    tiles = [tile for vector in held for parts in vector for tile in parts] + [note]
    for k, tile in enumerate(tiles):
        for chip in range(out.shape[0]):
            out[chip, k] = tile


def outputs_kernel(place, sums, gathered, others, modulus, residual):
    core = place[0]
    chips = gathered.shape[0]
    total = sums[0]
    for k in range(1, sums.shape[0]):
        total = total + sums[k]
    total = jnp.broadcast_to(jnp.sum(total, axis=1, keepdims=True), total.shape)
    m0, m1, m2, m3 = (total[k : k + 1] for k in range(4))
    step = m0 / m1
    norm = step * step * m2 - m0
    grown = 1.0 + norm / m0
    curve = grown * grown * m1 - 2.0 * step * grown * m2 + step * step * m3
    second = norm / curve
    shape = (chips, ROWS, total.shape[-1])
    p = jnp.broadcast_to((step + second * grown).reshape(1, 1, -1), shape)
    q = jnp.broadcast_to((step * second).reshape(1, 1, -1), shape)
    for source, first in ((gathered, 2 * core), (others, 2 - 2 * core)):
        for part in range(2):
            for plane in range(2):
                v0, v1, v2 = (source[:, 4 * k + 2 * part + plane] for k in range(3))
                flat = (chips * ROWS, shape[-1])
                modulus[part, first + plane] = (p * v0 - q * v1).reshape(flat)
                residual[part, first + plane] = (v0 - p * v1 + q * v2).reshape(flat)


def run(kernel, shapes, *arrays, scratch=(), scalars=1):
    vmem = pl.BlockSpec(memory_space=pltpu.VMEM)
    smem = pl.BlockSpec(memory_space=pltpu.SMEM)
    return pl.pallas_call(
        kernel,
        out_shape=shapes,
        in_specs=[smem] * scalars + [vmem] * (len(arrays) - scalars),
        out_specs=jax.tree.map(lambda _: vmem, shapes),
        scratch_shapes=list(scratch),
        compiler_params=pltpu.CompilerParams(vmem_limit_bytes=VMEM_BYTES),
    )(*arrays)


def body(displacement, freq_index, tissue):
    core = lax.axis_index("freq") % 2
    chips = lax.axis_size("freq") // 2
    slabs = lax.axis_size("gz")
    low = core == 0
    ny, nx = displacement.shape[-2:]
    tile = (ROWS, nx)
    place = jnp.stack([core, (low & (lax.axis_index("gz") == 0)).astype(jnp.int32)])

    def shape(*dims):
        return jax.ShapeDtypeStruct(dims, jnp.float32)

    field = displacement[0]
    first, last = (field[:, :, k].reshape(6, ny, nx) for k in (0, 3))
    same = to_slabs(jnp.where(low, last, first), 0, 0)
    cross = to_slabs(jnp.concatenate([jnp.where(low, first, last), tissue[:1].astype(jnp.float32)]), 1, 1)
    other = swap_cores(displacement)[0]
    other_index = swap_cores(freq_index)

    held = (place, freq_index, other_index, field, other, tissue)
    scratch = [pltpu.VMEM((15, ny + 2 * ROWS, nx), jnp.float32)]
    inner = run(inner_kernel, shape(chips, PLANE, *tile), *held, scratch=scratch, scalars=3)
    parts = run(outer_kernel, shape(chips, 2 * PLANE, *tile), *held, same, cross, inner, scratch=scratch, scalars=3)
    mine = over_chips(parts).sum(axis=0).reshape(2, PLANE, *tile)

    near = swap_cores(jnp.concatenate([mine[0], mine[1, :BEYOND]]))
    far = to_slabs(jnp.concatenate([mine[1], mine[0, :BEYOND]]), 1, 1)
    tiles = run(vectors_kernel, shape(chips, 13, *tile), place, mine, near, far)

    gathered = over_chips(tiles)
    sums = gathered[:, 12, :4].sum(axis=0)
    sums, gathered = lax.optimization_barrier((sums + swap_cores(sums), gathered))
    others = swap_cores(gathered)
    sums = lax.all_to_all(jnp.broadcast_to(sums, (slabs, *sums.shape)), "gz", split_axis=0, concat_axis=0, tiled=True)
    result = shape(2, 4, ny, nx)
    return tuple(run(outputs_kernel, (result, result), place, sums, gathered, others))


def solution(mesh):
    placed = (P("freq", None, None, "gz", None, None), P("freq"), P("gz", None, None))
    return jax.shard_map(
        body,
        mesh=mesh,
        in_specs=placed,
        out_specs=(P(None, "gz", None, None), P(None, "gz", None, None)),
        check_vma=False,
    )
```
